256 devices in a mesh: row: 32 (over z, y_lo, core), col: 8 (over y_hi, x).
Axes of the slice: x: 4, y: 4 (y_hi: 2, y_lo: 2; y = y_hi * 2 + y_lo), z: 8, core: 2. Of those that a mesh axis runs over, the one named last changes fastest.
Arguments:
- eigvec: float32 [65536, 4096], P('row', 'col'), may hold values from -6 to 6
- reflectors: float32 [32, 8, 1024, 256], P('row', 'col'), may hold values from -0.125 to 0.125
- tfactors: float32 [32, 8, 256, 256], P('row', 'col'), may hold values from -1 to 1, as said below
- offsets: int32 [2, 32], replicated, may hold values from 1024 to 1536
- owners: int32 [2, 32], replicated, may hold values from 0 to 7
Outputs:
- result: float32 [65536, 4096], P('row', 'col')
The draws below stay inside these ranges and needn't reach their ends.
Inputs may be any that keep to these rules, and one draw needn't show every extreme that they name: `tfactors`: every factor block is zero below its diagonal.
All inputs are finite; a program needn't handle non-finite values.
Results may differ from the reference program's by a relative error of at most 0.0003.
Values sent between devices are 32-bit elements; how exact they have to be, the bound alone decides.
No kernel may reach another device: no remote copies, remote signals or barrier semaphores. Data moves between devices by JAX's collectives and lax.ppermute only.
A program may use at most 64 MiB of HBM per device.

```python
import jax
import jax.numpy as jnp
from jax import lax

ORDER = 65536
WIN = 1024
BLOCK = 256
TICKS = 2
HALF = 512
ROWS_DEV = 2048
NCOLS = 4096
N_ROW = 32
N_COL = 8


def draw_tfactors(key, part):
    key_diag, key_upper = jax.random.split(jax.random.fold_in(key, 11))
    diagonal = jax.random.uniform(key_diag, (N_ROW, N_COL, BLOCK), jnp.float32, 0.3, 1.0)
    off_scale = 0.6
    entries = jax.random.normal(key_upper, (N_ROW, N_COL, BLOCK, BLOCK), jnp.float32) * (off_scale / BLOCK ** 0.5)
    positions = jnp.arange(BLOCK)
    strict_mask = positions[:, None] < positions[None, :]
    identity = (positions[:, None] == positions[None, :]).astype(jnp.float32)
    return jnp.where(strict_mask, entries, 0.0) + diagonal[..., None] * identity


def plant(result, rng, smallest, top_value):
    longest = result.shape.index(max(result.shape))
    spots = []
    for shift in (0, 1):
        where = [jax.random.randint(jax.random.fold_in(rng, axis), (), 0, length) for axis, length in enumerate(result.shape)]
        where[longest] = (where[longest] + shift) % result.shape[longest]
        spots.append(tuple(where))
    return result.at[spots[0]].set(smallest).at[spots[1]].set(top_value)


def steps_of(own_key, extent, cuts, least, high):
    loudness, own = 1.0, jax.random.fold_in(own_key, 6)
    for dim, parts in cuts:
        draws = jnp.exp(jax.random.uniform(jax.random.fold_in(own, dim), (parts,), jnp.float32, least / len(cuts), high / len(cuts)))
        loudness = loudness * jnp.repeat(draws, extent[dim] // parts).reshape([-1 if axis == dim else 1 for axis in range(len(extent))])
    return loudness


def bell_draw(stream_key, extent, scale, most, cuts=(), kind=jnp.bfloat16):
    level = steps_of(stream_key, extent, cuts, -0.22, 0.18) if cuts else 1.0
    array = jax.random.normal(stream_key, extent, jnp.float32) * scale * level
    return jnp.minimum(jnp.maximum(array, -most), most).astype(kind)


def setup_inputs(seed: int = 0) -> dict:
    key_of = jax.random.split(jax.random.key(seed), 6)
    return {
        "eigvec": bell_draw(key_of[0], (ORDER, NCOLS), 1.0, 6.0, ((0, 32), (1, 8)), jnp.float32),
        "reflectors": bell_draw(key_of[1], (N_ROW, N_COL, WIN, BLOCK), (2 * WIN) ** -0.5, 0.125, ((0, 32), (1, 8)), jnp.float32),
        "tfactors": draw_tfactors(jax.random.fold_in(key_of[5], 71), 0),
        "offsets": plant(jax.random.randint(key_of[3], (TICKS, N_ROW), ROWS_DEV - WIN, ROWS_DEV - HALF + 1), jax.random.fold_in(key_of[3], 1), ROWS_DEV - WIN, ROWS_DEV - HALF).astype(jnp.int32),
        "owners": plant(jax.random.randint(key_of[4], (TICKS, N_ROW), 0, N_COL), jax.random.fold_in(key_of[4], 1), 0, N_COL - 1).astype(jnp.int32),
    }


def project(vectors, window):
    return lax.dot_general(vectors, window, (((0,), (0,)), ((), ())), precision=lax.Precision.HIGHEST, preferred_element_type=jnp.float32)


def reference(eigvec, reflectors, tfactors, offsets, owners):
    row_count = ORDER // N_ROW
    half_rows = WIN // 2
    matrix = jnp.concatenate([eigvec, jnp.zeros((half_rows, eigvec.shape[1]), eigvec.dtype)], 0)
    for turn_index in range(TICKS):
        def update_slab(matrix, slab_index):
            begin_row = (slab_index * row_count + offsets[turn_index, slab_index]).astype(jnp.int32)
            source = owners[turn_index, slab_index]
            vector_block = reflectors[slab_index, source]
            factor_block = tfactors[slab_index, source]
            window = lax.dynamic_slice_in_dim(matrix, begin_row, WIN, 0)
            coefficients = project(vector_block, window)
            scaled = jnp.dot(factor_block, coefficients, precision=lax.Precision.HIGHEST, preferred_element_type=jnp.float32)
            window = window - jnp.dot(vector_block, scaled, precision=lax.Precision.HIGHEST, preferred_element_type=jnp.float32)
            return lax.dynamic_update_slice_in_dim(matrix, window, begin_row, 0), None

        matrix, unused = lax.scan(update_slab, matrix, jnp.arange(N_ROW, dtype=jnp.int32))
    return matrix[:ORDER]
```

```python
import jax
import jax.numpy as jnp
from jax import lax
from jax.experimental import pallas as pl
from jax.experimental.pallas import tpu as pltpu
from jax.sharding import PartitionSpec as P

WIN = 1024
HALF = 512
BLOCK = 256
TICKS = 2
PIECES = 8
VROWS = WIN // PIECES
TROWS = 24
PROWS = VROWS + TROWS
SPAN = WIN + 16
F32 = jnp.float32
BF16 = jnp.bfloat16


def split(x):
    hi = x.astype(BF16)
    return hi, (x - hi.astype(F32)).astype(BF16)


def mm(a, b, dims):
    return lax.dot_general(a, b, (dims, ((), ())), preferred_element_type=F32)


def mm3(ah, al, bh, bl, dims):
    return mm(ah, bh, dims) + mm(ah, bl, dims) + mm(al, bh, dims)


NN = ((1,), (0,))
TN = ((0,), (0,))


def update_kernel(idx, eig, halo, p, r, l, q, a, b, e, f, out, bottom, ext, vp, vh, vl, tf, wh, wl, sems):
    rows = eig.shape[0]
    load = pltpu.make_async_copy(eig.at[pl.ds(rows - WIN, WIN)], ext.at[pl.ds(0, WIN)], sems.at[0])
    keep = pltpu.make_async_copy(eig.at[pl.ds(HALF, rows - WIN - HALF)], out.at[pl.ds(HALF, rows - WIN - HALF)], sems.at[1])
    load.start()
    keep.start()
    ext[WIN : WIN + HALF, :] = halo[...]
    ext[WIN + HALF :, :] = jnp.zeros((16, ext.shape[1]), F32)
    for tick in range(TICKS):
        vp[tick, :8, :] = jnp.zeros((8, BLOCK), F32)
        vp[tick, WIN + 8 :, :] = jnp.zeros((16, BLOCK), F32)
    found = (
        (p, (0, PROWS)),
        (r, (0, PROWS)),
        (l, (0, PROWS)),
        (q, (0, PROWS)),
        (None, ((a, 0), (b, 0))),
        (a, (PROWS, 2 * PROWS)),
        (b, (PROWS, 2 * PROWS)),
        (None, ((e, 0), (f, 0))),
    )
    for tick in range(TICKS):
        for n, (ref, starts) in enumerate(found):
            src, at = starts[tick] if ref is None else (ref, starts[tick])
            k = idx[TICKS + n]
            vp[tick, pl.ds(pl.multiple_of(k * VROWS + 8, 8), VROWS), :] = src[at : at + VROWS, :]
            tf[tick, pl.ds(pl.multiple_of(k * TROWS, TROWS), TROWS), :] = src[at + VROWS : at + PROWS, :]
    for tick in range(TICKS):
        shift = idx[tick] % 8
        tiles = pltpu.roll(vp[tick].reshape(SPAN // 8 + 1, 8, BLOCK), shift, 1)
        same = lax.broadcasted_iota(jnp.int32, (SPAN // 8, 8, BLOCK), 1) >= shift
        hi, lo = split(jnp.where(same, tiles[1:], tiles[:-1]).reshape(SPAN, BLOCK))
        vh[tick] = hi
        vl[tick] = lo
    load.wait()
    for tick in range(TICKS):
        base = pl.multiple_of(idx[tick] // 8 * 8, 8)
        low = tf[tick, 128:192, :]
        corner = jnp.concatenate([low[:, :128], low[:, 128:]], 0)
        factor = jnp.concatenate([tf[tick, :128, :], jnp.concatenate([jnp.zeros((128, 128), F32), corner], 1)], 0)
        fh, fl = split(factor)
        hi, lo = split(ext[pl.ds(base, SPAN), :])
        wh[...] = hi
        wl[...] = lo
        coef = mm3(vh[tick], vl[tick], wh[...], wl[...], TN)
        ch, cl = split(coef)
        sh, sl = split(mm3(fh, fl, ch, cl, NN))
        for k in range(5):
            part = slice(k * 208, (k + 1) * 208)
            spot = pl.ds(pl.multiple_of(base + k * 208, 8), 208)
            ext[spot, :] = ext[spot, :] - mm3(vh[tick, part, :], vl[tick, part, :], sh, sl, NN)
    bottom[...] = ext[WIN : WIN + HALF, :]
    store = pltpu.make_async_copy(ext.at[pl.ds(0, WIN)], out.at[pl.ds(rows - WIN, WIN)], sems.at[2])
    store.start()
    keep.wait()
    store.wait()


def update(idx, eig, halo, pieces):
    vmem = pl.BlockSpec(memory_space=pltpu.VMEM)
    hbm = pl.BlockSpec(memory_space=pl.ANY)
    columns = eig.shape[1]
    return pl.pallas_call(
        update_kernel,
        out_shape=(
            jax.ShapeDtypeStruct(eig.shape, F32),
            jax.ShapeDtypeStruct((HALF, columns), F32),
        ),
        in_specs=[pl.BlockSpec(memory_space=pltpu.SMEM), hbm] + [vmem] * 9,
        out_specs=(hbm, vmem),
        scratch_shapes=[
            pltpu.VMEM((WIN + HALF + 16, columns), F32),
            pltpu.VMEM((TICKS, SPAN + 8, BLOCK), F32),
            pltpu.VMEM((TICKS, SPAN, BLOCK), BF16),
            pltpu.VMEM((TICKS, SPAN, BLOCK), BF16),
            pltpu.VMEM((TICKS, 192, BLOCK), F32),
            pltpu.VMEM((SPAN, columns), BF16),
            pltpu.VMEM((SPAN, columns), BF16),
            pltpu.SemaphoreType.DMA((3,)),
        ],
        compiler_params=pltpu.CompilerParams(vmem_limit_bytes=40 * 1024 * 1024),
        cost_estimate=pl.CostEstimate(flops=8_000_000_000, bytes_accessed=16_000_000, transcendentals=0),
        name="update",
    )(idx, eig, halo, *pieces)


def per_device(eigvec, reflectors, tfactors, offsets, owners):
    rows = eigvec.shape[0]
    row = lax.axis_index("row")
    col = lax.axis_index("col")
    y, x = col // 4, col % 4
    count = lax.axis_size("row")

    halo = lax.ppermute(eigvec[:HALF], "row", [(i + 1, i) for i in range(count - 1)])

    vectors = reflectors[0, 0].reshape(PIECES, VROWS, BLOCK)
    factor = tfactors[0, 0]
    packed = jnp.concatenate([factor[:128], jnp.concatenate([factor[128:192, 128:], factor[192:, 128:]], 1)], 0)
    block = jnp.concatenate([vectors, packed.reshape(PIECES, TROWS, BLOCK)], 1)
    mine = lax.all_to_all(block, "col", 0, 0)
    source = lax.dynamic_slice_in_dim(owners, row, 1, 1)[:, 0]
    begin = lax.dynamic_slice_in_dim(offsets, row, 1, 1)[:, 0]
    p = jnp.concatenate([lax.dynamic_index_in_dim(mine, source[t], 0, keepdims=False) for t in range(TICKS)], 0)

    def from_x(value, d):
        return lax.ppermute(value, "col", [((i // 4) * 4 + (i % 4 + d) % 4, i) for i in range(8)])

    r, l = from_x(p, 1), from_x(p, -1)
    q = lax.ppermute(p, "col", [(i, i ^ 4) for i in range(8)])
    a = from_x(jnp.concatenate([r[:PROWS], q], 0), 1)
    b = from_x(jnp.concatenate([l[PROWS:], q], 0), -1)
    e = from_x(a[PROWS : 2 * PROWS], 1)
    f = from_x(b[2 * PROWS :], -1)

    here, there = 4 * y, 4 * (1 - y)
    right, left, across = (x + 1) % 4, (x + 3) % 4, (x + 2) % 4
    order = [here + x, here + right, here + left, there + x, here + across, there + right, there + left, there + across]
    idx = jnp.stack([begin[0] - WIN, begin[1] - WIN] + order).astype(jnp.int32)

    out, bottom = update(idx, eigvec, halo, (p, r, l, q, a, b, e, f))
    upper = lax.ppermute(bottom, "row", [(i, i + 1) for i in range(count - 1)])
    top = jnp.where(row > 0, upper, eigvec[:HALF])
    return lax.dynamic_update_slice_in_dim(out, top, 0, 0)


def solution(mesh):
    return jax.shard_map(
        per_device,
        mesh=mesh,
        in_specs=(
            P("row", "col"),
            P("row", "col", None, None),
            P("row", "col", None, None),
            P(),
            P(),
        ),
        out_specs=P("row", "col"),
        check_vma=False,
    )
```

```python
import jax
import jax.numpy as jnp
from jax import lax
from jax.experimental import pallas as pl
from jax.experimental.pallas import tpu as pltpu
from jax.sharding import PartitionSpec as P

WIN = 1024
HALF = 512
BLOCK = 256
TICKS = 2
PIECES = 8
VROWS = WIN // PIECES
TROWS = 24
PROWS = VROWS + TROWS
SPAN = WIN + 16
EXT = WIN + HALF + 16
MIB = 1024 * 1024
F32 = jnp.float32
BF16 = jnp.bfloat16
NN = ((1,), (0,))
TN = ((0,), (0,))

SMEM = pl.BlockSpec(memory_space=pltpu.SMEM)
VMEM = pl.BlockSpec(memory_space=pltpu.VMEM)
HBM = pl.BlockSpec(memory_space=pltpu.HBM)


def split(x):
    hi = x.astype(BF16)
    return hi, (x - hi.astype(F32)).astype(BF16)


def mm(a, b, dims):
    return lax.dot_general(a, b, (dims, ((), ())), preferred_element_type=F32)


def mm3(ah, al, bh, bl, dims):
    return mm(ah, bh, dims) + mm(ah, bl, dims) + mm(al, bh, dims)


def hbm(*arrays):
    return [pltpu.with_memory_space_constraint(a, pltpu.HBM) for a in arrays]


def vmem(*arrays):
    return [pltpu.with_memory_space_constraint(a, pltpu.VMEM) for a in arrays]


def cost(flops, moved):
    return pl.CostEstimate(flops=flops, bytes_accessed=moved, transcendentals=0)


def pack_kernel(vectors, factor, block, sems):
    copies = []
    for k in range(PIECES):
        pairs = (
            (vectors.at[0, 0, pl.ds(k * VROWS, VROWS)], block.at[k, pl.ds(0, VROWS)]),
            (factor.at[0, 0, pl.ds(k * 16, 16)], block.at[k, pl.ds(VROWS, 16)]),
            (factor.at[0, 0, pl.ds(128 + k * 8, 8), pl.ds(128, 128)], block.at[k, pl.ds(VROWS + 16, 8), pl.ds(0, 128)]),
            (factor.at[0, 0, pl.ds(192 + k * 8, 8), pl.ds(128, 128)], block.at[k, pl.ds(VROWS + 16, 8), pl.ds(128, 128)]),
        )
        for n, (src, dst) in enumerate(pairs):
            copies.append(pltpu.make_async_copy(src, dst, sems.at[k, n]))
    for copy in copies:
        copy.start()
    for copy in copies:
        copy.wait()


def pack(reflectors, tfactors):
    return pl.pallas_call(
        pack_kernel,
        out_shape=pltpu.VMEM((PIECES, PROWS, BLOCK), F32),
        in_specs=[HBM, HBM],
        out_specs=VMEM,
        scratch_shapes=[pltpu.SemaphoreType.DMA((PIECES, 4))],
        compiler_params=pltpu.CompilerParams(vmem_limit_bytes=4 * MIB),
        cost_estimate=cost(0, 3 * MIB),
        name="pack",
    )(*hbm(reflectors, tfactors))


def load_kernel(eig, ext, sem):
    copy = pltpu.make_async_copy(eig.at[pl.ds(eig.shape[0] - WIN, WIN)], ext.at[pl.ds(0, WIN)], sem)
    copy.start()
    copy.wait()


def load(eig):
    return pl.pallas_call(
        load_kernel,
        out_shape=pltpu.VMEM((EXT, eig.shape[1]), F32),
        in_specs=[HBM],
        out_specs=VMEM,
        scratch_shapes=[pltpu.SemaphoreType.DMA],
        compiler_params=pltpu.CompilerParams(vmem_limit_bytes=4 * MIB),
        cost_estimate=cost(0, 4 * MIB),
        name="load",
    )(*hbm(eig))


def head_kernel(eig, *refs):
    copy = pltpu.make_async_copy(eig.at[pl.ds(0, HALF)], refs[-2], refs[-1])
    copy.start()
    copy.wait()


def head(eig, after):
    return pl.pallas_call(
        head_kernel,
        out_shape=pltpu.VMEM((HALF, eig.shape[1]), F32),
        in_specs=[HBM] + [pl.BlockSpec(memory_space=pl.ANY)] * len(after),
        out_specs=VMEM,
        scratch_shapes=[pltpu.SemaphoreType.DMA],
        compiler_params=pltpu.CompilerParams(vmem_limit_bytes=4 * MIB),
        cost_estimate=cost(0, 2 * MIB),
        name="head",
    )(*hbm(eig), *after)


def update_kernel(where, offsets, start, halo, p, r, l, s, q, u, v, z, ext, bottom, vp, vh, vl, tf, wh, wl):
    row, col = where[0], where[1]
    x, here = col & 3, col & 4
    there = 4 - here
    right, left, across = (x + 1) & 3, (x + 3) & 3, (x + 2) & 3
    places = (here + x, here + right, here + left, here + across, there + x, there + right, there + left, there + across)
    ext[WIN : WIN + HALF, :] = halo[...]
    ext[WIN + HALF :, :] = jnp.zeros((EXT - WIN - HALF, ext.shape[1]), F32)
    for tick in range(TICKS):
        vp[tick, :8, :] = jnp.zeros((8, BLOCK), F32)
        vp[tick, WIN + 8 :, :] = jnp.zeros((16, BLOCK), F32)
        tf[tick, 128:, :128] = jnp.zeros((128, 128), F32)
        at = tick * PROWS
        for ref, k in zip((p, r, l, s, q, u, v, z), places):
            vp[tick, pl.ds(pl.multiple_of(k * VROWS + 8, 8), VROWS), :] = ref[at : at + VROWS, :]
            at16, at8 = at + VROWS, at + VROWS + 16
            tf[tick, pl.ds(pl.multiple_of(k * 16, 16), 16), :] = ref[at16 : at16 + 16, :]
            tf[tick, pl.ds(pl.multiple_of(128 + k * 8, 8), 8), 128:] = ref[at8 : at8 + 8, :128]
            tf[tick, pl.ds(pl.multiple_of(192 + k * 8, 8), 8), 128:] = ref[at8 : at8 + 8, 128:]
    for tick in range(TICKS):
        shift = offsets[tick, row] & 7
        tiles = pltpu.roll(vp[tick].reshape(SPAN // 8 + 1, 8, BLOCK), shift, 1)
        same = lax.broadcasted_iota(jnp.int32, (SPAN // 8, 8, BLOCK), 1) >= shift
        hi, lo = split(jnp.where(same, tiles[1:], tiles[:-1]).reshape(SPAN, BLOCK))
        vh[tick] = hi
        vl[tick] = lo
    for tick in range(TICKS):
        base = pl.multiple_of((offsets[tick, row] - WIN) >> 3 << 3, 8)
        fh, fl = split(tf[tick])
        hi, lo = split(ext[pl.ds(base, SPAN), :])
        wh[...] = hi
        wl[...] = lo
        ch, cl = split(mm3(vh[tick], vl[tick], wh[...], wl[...], TN))
        sh, sl = split(mm3(fh, fl, ch, cl, NN))
        for k in range(5):
            part = slice(k * 208, (k + 1) * 208)
            spot = pl.ds(pl.multiple_of(base + k * 208, 8), 208)
            ext[spot, :] = ext[spot, :] - mm3(vh[tick, part, :], vl[tick, part, :], sh, sl, NN)
    bottom[...] = ext[WIN : WIN + HALF, :]


def update(where, offsets, start, halo, pieces):
    columns = start.shape[1]
    return pl.pallas_call(
        update_kernel,
        out_shape=(pltpu.VMEM((EXT, columns), F32), pltpu.VMEM((HALF, columns), F32)),
        in_specs=[SMEM, SMEM] + [VMEM] * 10,
        out_specs=(VMEM, VMEM),
        input_output_aliases={2: 0},
        scratch_shapes=[
            pltpu.VMEM((TICKS, SPAN + 8, BLOCK), F32),
            pltpu.VMEM((TICKS, SPAN, BLOCK), BF16),
            pltpu.VMEM((TICKS, SPAN, BLOCK), BF16),
            pltpu.VMEM((TICKS, BLOCK, BLOCK), F32),
            pltpu.VMEM((SPAN, columns), BF16),
            pltpu.VMEM((SPAN, columns), BF16),
        ],
        compiler_params=pltpu.CompilerParams(vmem_limit_bytes=20 * MIB),
        cost_estimate=cost(6_000_000_000, 8 * MIB),
        name="update",
    )(where, offsets, *vmem(start), halo, *pieces)


def store_kernel(eig, ext, out, sems):
    rows = eig.shape[0]
    middle = pl.ds(HALF, rows - WIN - HALF)
    keep = pltpu.make_async_copy(eig.at[middle], out.at[middle], sems.at[0])
    store = pltpu.make_async_copy(ext.at[pl.ds(0, WIN)], out.at[pl.ds(rows - WIN, WIN)], sems.at[1])
    keep.start()
    store.start()
    keep.wait()
    store.wait()


def store(eig, ext):
    return pl.pallas_call(
        store_kernel,
        out_shape=pltpu.HBM(eig.shape, F32),
        in_specs=[HBM, VMEM],
        out_specs=HBM,
        scratch_shapes=[pltpu.SemaphoreType.DMA((2,))],
        compiler_params=pltpu.CompilerParams(vmem_limit_bytes=8 * MIB),
        cost_estimate=cost(0, 8 * MIB),
        name="store",
    )(*hbm(eig), *vmem(ext))


def finish_kernel(where, eig, upper, old, out, sem):
    head = out.at[pl.ds(0, HALF)]

    @pl.when(where[0] > 0)
    def _():
        copy = pltpu.make_async_copy(upper, head, sem)
        copy.start()
        copy.wait()

    @pl.when(where[0] == 0)
    def _():
        copy = pltpu.make_async_copy(eig.at[pl.ds(0, HALF)], head, sem)
        copy.start()
        copy.wait()


def finish(where, eig, upper, out):
    return pl.pallas_call(
        finish_kernel,
        out_shape=pltpu.HBM(eig.shape, F32),
        in_specs=[SMEM, HBM, VMEM, HBM],
        out_specs=HBM,
        input_output_aliases={3: 0},
        scratch_shapes=[pltpu.SemaphoreType.DMA],
        compiler_params=pltpu.CompilerParams(vmem_limit_bytes=4 * MIB),
        cost_estimate=cost(0, 2 * MIB),
        name="finish",
    )(where, *hbm(eig), *vmem(upper), *hbm(out))


def per_device(eigvec, reflectors, tfactors, offsets, owners):
    row = lax.axis_index("row")
    col = lax.axis_index("col")
    where = jnp.stack([row, col]).astype(jnp.int32)
    count = lax.axis_size("row")
    source = lax.dynamic_slice_in_dim(owners, row, 1, 1)[:, 0]

    def from_x(value, d):
        return lax.ppermute(value, "col", [((i // 4) * 4 + (i % 4 + d) % 4, i) for i in range(8)])

    def from_y(value):
        return lax.ppermute(value, "col", [(i, i ^ 4) for i in range(8)])

    mine = lax.all_to_all(pack(reflectors, tfactors), "col", 0, 0)
    start = load(eigvec)
    p = jnp.concatenate([lax.dynamic_index_in_dim(mine, source[t], 0, keepdims=False) for t in range(TICKS)], 0)
    q, s, r, l = from_y(p), from_x(p, 2), from_x(p, 1), from_x(p, -1)
    u, v, z = from_x(q, 1), from_x(q, -1), from_y(s)
    top = head(eigvec, (q, s, r, l))
    halo = lax.ppermute(top, "row", [(i + 1, i) for i in range(count - 1)])

    ext, bottom = update(where, offsets, start, halo, (p, r, l, s, q, u, v, z))
    upper = lax.ppermute(bottom, "row", [(i, i + 1) for i in range(count - 1)])
    return finish(where, eigvec, upper, store(eigvec, ext))


def solution(mesh):
    return jax.shard_map(
        per_device,
        mesh=mesh,
        in_specs=(
            P("row", "col"),
            P("row", "col", None, None),
            P("row", "col", None, None),
            P(),
            P(),
        ),
        out_specs=P("row", "col"),
        check_vma=False,
    )
```

```python
import jax
import jax.numpy as jnp
from jax import lax
from jax.experimental import pallas as pl
from jax.experimental.pallas import tpu as pltpu
from jax.sharding import PartitionSpec as P

WIN = 1024
HALF = 512
BLOCK = 256
TICKS = 2
PIECES = 8
VROWS = WIN // PIECES
TROWS = 24
PROWS = VROWS + TROWS
SPAN = WIN + 16
REACH = WIN + HALF
MIB = 1024 * 1024
F32 = jnp.float32
BF16 = jnp.bfloat16
NN = ((1,), (0,))
TN = ((0,), (0,))

SMEM = pl.BlockSpec(memory_space=pltpu.SMEM)
VMEM = pl.BlockSpec(memory_space=pltpu.VMEM)
ANY = pl.BlockSpec(memory_space=pl.ANY)
HBM = pl.BlockSpec(memory_space=pltpu.HBM)


def split(x):
    hi = x.astype(BF16)
    return hi, (x - hi.astype(F32)).astype(BF16)


def mm(a, b, dims):
    return lax.dot_general(a, b, (dims, ((), ())), preferred_element_type=F32)


def mm3(ah, al, bh, bl, dims):
    return mm(ah, bh, dims) + mm(ah, bl, dims) + mm(al, bh, dims)


def hbm(*arrays):
    return [pltpu.with_memory_space_constraint(a, pltpu.HBM) for a in arrays]


def vmem(*arrays):
    return [pltpu.with_memory_space_constraint(a, pltpu.VMEM) for a in arrays]


def cost(flops, moved):
    return pl.CostEstimate(flops=flops, bytes_accessed=moved, transcendentals=0)


def pack_kernel(vectors, factor, eig, block, top, sems, first):
    lead = pltpu.make_async_copy(eig.at[pl.ds(0, HALF)], top, first)
    lead.start()
    copies = []
    for k in range(PIECES):
        pairs = (
            (vectors.at[0, 0, pl.ds(k * VROWS, VROWS)], block.at[k, pl.ds(0, VROWS)]),
            (factor.at[0, 0, pl.ds(k * 16, 16)], block.at[k, pl.ds(VROWS, 16)]),
            (factor.at[0, 0, pl.ds(128 + k * 8, 8), pl.ds(128, 128)], block.at[k, pl.ds(VROWS + 16, 8), pl.ds(0, 128)]),
            (factor.at[0, 0, pl.ds(192 + k * 8, 8), pl.ds(128, 128)], block.at[k, pl.ds(VROWS + 16, 8), pl.ds(128, 128)]),
        )
        for n, (src, dst) in enumerate(pairs):
            copies.append(pltpu.make_async_copy(src, dst, sems.at[k, n]))
    for copy in copies:
        copy.start()
    lead.wait()
    for copy in copies:
        copy.wait()


def pack(reflectors, tfactors, eig):
    return pl.pallas_call(
        pack_kernel,
        out_shape=(jax.ShapeDtypeStruct((PIECES, PROWS, BLOCK), F32), jax.ShapeDtypeStruct((HALF, eig.shape[1]), F32)),
        in_specs=[HBM, HBM, HBM],
        out_specs=(VMEM, VMEM),
        scratch_shapes=[pltpu.SemaphoreType.DMA((PIECES, 4)), pltpu.SemaphoreType.DMA],
        compiler_params=pltpu.CompilerParams(vmem_limit_bytes=6 * MIB),
        cost_estimate=cost(0, 5 * MIB),
        name="pack",
    )(*hbm(reflectors, tfactors, eig))


def stage_kernel(eig, halo, wh, wl, rows, sems):
    upper = pltpu.make_async_copy(eig.at[pl.ds(eig.shape[0] - WIN, WIN)], rows.at[pl.ds(0, WIN)], sems.at[0])
    lower = pltpu.make_async_copy(halo, rows.at[pl.ds(WIN, HALF)], sems.at[1])
    upper.start()
    lower.start()
    upper.wait()
    lower.wait()
    wh[...], wl[...] = split(rows[...])


def stage(eig, halo):
    columns = eig.shape[1]
    return pl.pallas_call(
        stage_kernel,
        out_shape=(jax.ShapeDtypeStruct((REACH, columns), BF16), jax.ShapeDtypeStruct((REACH, columns), BF16)),
        in_specs=[HBM, ANY],
        out_specs=(VMEM, VMEM),
        scratch_shapes=[pltpu.VMEM((REACH, columns), F32), pltpu.SemaphoreType.DMA((2,))],
        compiler_params=pltpu.CompilerParams(vmem_limit_bytes=10 * MIB),
        cost_estimate=cost(0, 9 * MIB),
        name="stage",
    )(*hbm(eig), halo)


def update_kernel(where, offsets, wh, wl, halo, p, r, l, s, q, u, v, z, bottom, vh, vl, sh, sl, vp, tp, va, low, sems, last):
    row, col = where[0], where[1]
    x, here = col & 3, col & 4
    there = 4 - here
    right, left, across = (x + 1) & 3, (x + 3) & 3, (x + 2) & 3
    places = (here + x, here + right, here + left, here + across, there + x, there + right, there + left, there + across)
    copies = []
    for tick in range(TICKS):
        for n, (ref, k) in enumerate(zip((p, r, l, s, q, u, v, z), places)):
            spot = pl.ds(pl.multiple_of(k * VROWS + 8, 8), VROWS)
            copies.append(pltpu.make_async_copy(ref.at[pl.ds(tick * PROWS, VROWS)], vp.at[tick, spot], sems.at[tick, n, 0]))
            spot = pl.ds(pl.multiple_of(k * TROWS, 8), TROWS)
            copies.append(pltpu.make_async_copy(ref.at[pl.ds(tick * PROWS + VROWS, TROWS)], tp.at[tick, spot], sems.at[tick, n, 1]))
    for copy in copies:
        copy.start()
    tail = pltpu.make_async_copy(halo, low, last)
    tail.start()
    for tick in range(TICKS):
        vp[tick, :8, :] = jnp.zeros((8, BLOCK), F32)
        vp[tick, WIN + 8 :, :] = jnp.zeros((16, BLOCK), F32)
        va[tick] = jnp.zeros((REACH + 16, BLOCK), F32)
    for copy in copies:
        copy.wait()
    factors = []
    for tick in range(TICKS):
        shift = offsets[tick, row] & 7
        base = pl.multiple_of((offsets[tick, row] - WIN) >> 3 << 3, 8)
        tiles = pltpu.roll(vp[tick].reshape(SPAN // 8 + 1, 8, BLOCK), shift, 1)
        same = lax.broadcasted_iota(jnp.int32, (SPAN // 8, 8, BLOCK), 1) >= shift
        va[tick, pl.ds(base, SPAN), :] = jnp.where(same, tiles[1:], tiles[:-1]).reshape(SPAN, BLOCK)
        part = slice(tick * BLOCK, (tick + 1) * BLOCK)
        vh[:, part], vl[:, part] = split(va[tick, :REACH, :])
        packed = tp[tick].reshape(PIECES, TROWS, BLOCK)
        corner = jnp.concatenate([packed[:, 16:, :128].reshape(64, 128), packed[:, 16:, 128:].reshape(64, 128)], 0)
        lower = jnp.concatenate([jnp.zeros((128, 128), F32), corner], 1)
        factors.append(split(jnp.concatenate([packed[:, :16, :].reshape(128, BLOCK), lower], 0)))
    coef = mm3(vh[...], vl[...], wh[...], wl[...], TN)
    cross = split(mm3(vh[:, BLOCK:], vl[:, BLOCK:], vh[:, :BLOCK], vl[:, :BLOCK], TN))
    first = split(mm3(*factors[0], *split(coef[:BLOCK]), NN))
    second = split(mm3(*factors[1], *split(coef[BLOCK:] - mm3(*cross, *first, NN)), NN))
    sh[:BLOCK, :], sl[:BLOCK, :] = first
    sh[BLOCK:, :], sl[BLOCK:, :] = second
    tail.wait()
    bottom[...] = low[...] - mm3(vh[WIN:, :], vl[WIN:, :], sh[...], sl[...], NN)


def update(where, offsets, wh, wl, halo, pieces):
    columns = halo.shape[1]
    both = TICKS * BLOCK
    return pl.pallas_call(
        update_kernel,
        out_shape=(
            jax.ShapeDtypeStruct((HALF, columns), F32),
            jax.ShapeDtypeStruct((REACH, both), BF16),
            jax.ShapeDtypeStruct((REACH, both), BF16),
            jax.ShapeDtypeStruct((both, columns), BF16),
            jax.ShapeDtypeStruct((both, columns), BF16),
        ),
        in_specs=[SMEM, SMEM, VMEM, VMEM] + [ANY] * 9,
        out_specs=(VMEM,) * 5,
        scratch_shapes=[
            pltpu.VMEM((TICKS, SPAN + 8, BLOCK), F32),
            pltpu.VMEM((TICKS, PIECES * TROWS, BLOCK), F32),
            pltpu.VMEM((TICKS, REACH + 16, BLOCK), F32),
            pltpu.VMEM((HALF, columns), F32),
            pltpu.SemaphoreType.DMA((TICKS, PIECES, 2)),
            pltpu.SemaphoreType.DMA,
        ],
        compiler_params=pltpu.CompilerParams(vmem_limit_bytes=24 * MIB),
        cost_estimate=cost(5_000_000_000, 8 * MIB),
        name="update",
    )(where, offsets, wh, wl, halo, *pieces)


def store_kernel(eig, vh, vl, sh, sl, out, rows, middle, sems):
    count = eig.shape[0]
    spot = pl.ds(HALF, count - WIN - HALF)
    load = pltpu.make_async_copy(eig.at[pl.ds(count - WIN, WIN)], rows, sems.at[0])
    fetch = pltpu.make_async_copy(eig.at[spot], middle, sems.at[1])
    load.start()
    fetch.start()
    fetch.wait()
    keep = pltpu.make_async_copy(middle, out.at[spot], sems.at[2])
    keep.start()
    load.wait()
    for k in range(4):
        part = slice(k * 256, (k + 1) * 256)
        rows[part, :] = rows[part, :] - mm3(vh[part, :], vl[part, :], sh[...], sl[...], NN)
    store = pltpu.make_async_copy(rows, out.at[pl.ds(count - WIN, WIN)], sems.at[3])
    store.start()
    keep.wait()
    store.wait()


def store(eig, vh, vl, sh, sl):
    columns = eig.shape[1]
    return pl.pallas_call(
        store_kernel,
        out_shape=jax.ShapeDtypeStruct(eig.shape, F32),
        in_specs=[HBM] + [VMEM] * 4,
        out_specs=HBM,
        scratch_shapes=[
            pltpu.VMEM((WIN, columns), F32),
            pltpu.VMEM((eig.shape[0] - WIN - HALF, columns), F32),
            pltpu.SemaphoreType.DMA((4,)),
        ],
        compiler_params=pltpu.CompilerParams(vmem_limit_bytes=16 * MIB),
        cost_estimate=cost(1_600_000_000, 8 * MIB),
        name="store",
    )(*hbm(eig), vh, vl, sh, sl)


def finish_kernel(where, eig, upper, old, out, rows, sems):
    head = out.at[pl.ds(0, HALF)]

    @pl.when(where[0] > 0)
    def _():
        copy = pltpu.make_async_copy(upper, head, sems.at[0])
        copy.start()
        copy.wait()

    @pl.when(where[0] == 0)
    def _():
        fetch = pltpu.make_async_copy(eig.at[pl.ds(0, HALF)], rows, sems.at[1])
        fetch.start()
        fetch.wait()
        copy = pltpu.make_async_copy(rows, head, sems.at[2])
        copy.start()
        copy.wait()


def finish(where, eig, upper, out):
    return pl.pallas_call(
        finish_kernel,
        out_shape=pltpu.HBM(eig.shape, F32),
        in_specs=[SMEM, HBM, VMEM, HBM],
        out_specs=HBM,
        input_output_aliases={3: 0},
        scratch_shapes=[pltpu.VMEM((HALF, eig.shape[1]), F32), pltpu.SemaphoreType.DMA((3,))],
        compiler_params=pltpu.CompilerParams(vmem_limit_bytes=4 * MIB),
        cost_estimate=cost(0, 2 * MIB),
        name="finish",
    )(where, *hbm(eig), *vmem(upper), *hbm(out))


def per_device(eigvec, reflectors, tfactors, offsets, owners):
    row = lax.axis_index("row")
    col = lax.axis_index("col")
    where = jnp.stack([row, col]).astype(jnp.int32)
    count = lax.axis_size("row")
    source = lax.dynamic_slice_in_dim(owners, row, 1, 1)[:, 0]

    def from_x(value, d):
        return lax.ppermute(value, "col", [((i // 4) * 4 + (i % 4 + d) % 4, i) for i in range(8)])

    def from_y(value):
        return lax.ppermute(value, "col", [(i, i ^ 4) for i in range(8)])

    block, top = pack(reflectors, tfactors, eigvec)
    halo = lax.ppermute(top, "row", [(i + 1, i) for i in range(count - 1)])
    mine = lax.all_to_all(block, "col", 0, 0)
    p = jnp.concatenate([lax.dynamic_index_in_dim(mine, source[t], 0, keepdims=False) for t in range(TICKS)], 0)
    q, s, r, l = from_y(p), from_x(p, 2), from_x(p, 1), from_x(p, -1)
    u, v, z = from_x(q, 1), from_x(q, -1), from_y(s)
    wh, wl = stage(eigvec, halo)

    bottom, *rest = update(where, offsets, wh, wl, halo, (p, r, l, s, q, u, v, z))
    upper = lax.ppermute(bottom, "row", [(i, i + 1) for i in range(count - 1)])
    return finish(where, eigvec, upper, store(eigvec, *rest))


def solution(mesh):
    return jax.shard_map(
        per_device,
        mesh=mesh,
        in_specs=(
            P("row", "col"),
            P("row", "col", None, None),
            P("row", "col", None, None),
            P(),
            P(),
        ),
        out_specs=P("row", "col"),
        check_vma=False,
    )
```

```python
import jax
import jax.numpy as jnp
from jax import lax
from jax.experimental import pallas as pl
from jax.experimental.pallas import tpu as pltpu
from jax.sharding import PartitionSpec as P

WIN = 1024
HALF = 512
BLOCK = 256
TICKS = 2
PIECES = 8
VROWS = WIN // PIECES
TROWS = 24
PROWS = VROWS + TROWS
SPAN = WIN + 16
REACH = WIN + HALF
MIB = 1024 * 1024
F32 = jnp.float32
BF16 = jnp.bfloat16
NN = ((1,), (0,))
TN = ((0,), (0,))

SMEM = pl.BlockSpec(memory_space=pltpu.SMEM)
VMEM = pl.BlockSpec(memory_space=pltpu.VMEM)
ANY = pl.BlockSpec(memory_space=pl.ANY)
HBM = pl.BlockSpec(memory_space=pltpu.HBM)


def split(x):
    hi = x.astype(BF16)
    return hi, (x - hi.astype(F32)).astype(BF16)


def mm(a, b, dims):
    return lax.dot_general(a, b, (dims, ((), ())), preferred_element_type=F32)


def mm3(ah, al, bh, bl, dims):
    return mm(ah, bh, dims) + mm(ah, bl, dims) + mm(al, bh, dims)


def hbm(*arrays):
    return [pltpu.with_memory_space_constraint(a, pltpu.HBM) for a in arrays]


def vmem(*arrays):
    return [pltpu.with_memory_space_constraint(a, pltpu.VMEM) for a in arrays]


def cost(flops, moved):
    return pl.CostEstimate(flops=flops, bytes_accessed=moved, transcendentals=0)


def pack_kernel(vectors, factor, eig, stay, right, across, left, top, sems, first):
    col = lax.axis_index("col")
    x, side = col & 3, col >> 2
    copies = []
    for n, out in enumerate((stay, right, across, left)):
        for half in range(2):
            k = 2 * ((x + n) & 3) + (side if half == 0 else 1 - side)
            at = half * PROWS
            pairs = (
                (vectors.at[0, 0, pl.ds(pl.multiple_of(k * VROWS, 8), VROWS)], out.at[pl.ds(at, VROWS)]),
                (factor.at[0, 0, pl.ds(pl.multiple_of(k * 16, 8), 16)], out.at[pl.ds(at + VROWS, 16)]),
                (
                    factor.at[0, 0, pl.ds(pl.multiple_of(128 + k * 8, 8), 8), pl.ds(128, 128)],
                    out.at[pl.ds(at + VROWS + 16, 8), pl.ds(0, 128)],
                ),
                (
                    factor.at[0, 0, pl.ds(pl.multiple_of(192 + k * 8, 8), 8), pl.ds(128, 128)],
                    out.at[pl.ds(at + VROWS + 16, 8), pl.ds(128, 128)],
                ),
            )
            for i, (src, dst) in enumerate(pairs):
                copies.append(pltpu.make_async_copy(src, dst, sems.at[n, half, i]))
    for copy in copies:
        copy.start()
    lead = pltpu.make_async_copy(eig.at[pl.ds(0, HALF)], top, first)
    lead.start()
    for copy in copies:
        copy.wait()
    lead.wait()


def pack(reflectors, tfactors, eig):
    quarter = jax.ShapeDtypeStruct((2 * PROWS, BLOCK), F32)
    return pl.pallas_call(
        pack_kernel,
        out_shape=(quarter,) * 4 + (jax.ShapeDtypeStruct((HALF, eig.shape[1]), F32),),
        in_specs=[HBM, HBM, HBM],
        out_specs=(VMEM,) * 5,
        scratch_shapes=[pltpu.SemaphoreType.DMA((4, 2, 4)), pltpu.SemaphoreType.DMA],
        compiler_params=pltpu.CompilerParams(vmem_limit_bytes=6 * MIB),
        cost_estimate=cost(0, 5 * MIB),
        name="pack",
    )(*hbm(reflectors, tfactors, eig))


def stage_kernel(eig, halo, wh, wl, rows, sems):
    upper = pltpu.make_async_copy(eig.at[pl.ds(eig.shape[0] - WIN, WIN)], rows.at[pl.ds(0, WIN)], sems.at[0])
    lower = pltpu.make_async_copy(halo, rows.at[pl.ds(WIN, HALF)], sems.at[1])
    upper.start()
    lower.start()
    upper.wait()
    lower.wait()
    wh[...], wl[...] = split(rows[...])


def stage(eig, halo):
    columns = eig.shape[1]
    return pl.pallas_call(
        stage_kernel,
        out_shape=(jax.ShapeDtypeStruct((REACH, columns), BF16), jax.ShapeDtypeStruct((REACH, columns), BF16)),
        in_specs=[HBM, ANY],
        out_specs=(VMEM, VMEM),
        scratch_shapes=[pltpu.VMEM((REACH, columns), F32), pltpu.SemaphoreType.DMA((2,))],
        compiler_params=pltpu.CompilerParams(vmem_limit_bytes=10 * MIB),
        cost_estimate=cost(0, 9 * MIB),
        name="stage",
    )(*hbm(eig), halo)


def choose_kernel(owners, stay, near, far, back, own, send):
    row, col = lax.axis_index("row"), lax.axis_index("col")
    for tick in range(TICKS):
        step = (owners[tick, row] - col) & 3
        part = slice(tick * PROWS, (tick + 1) * PROWS)
        for n, ref in enumerate((stay, near, far, back)):

            @pl.when(step == n)
            def _():
                own[part, :] = ref[:PROWS, :]
                send[part, :] = ref[PROWS:, :]


def choose(owners, arrived):
    half = jax.ShapeDtypeStruct((TICKS * PROWS, BLOCK), F32)
    return pl.pallas_call(
        choose_kernel,
        out_shape=(half, half),
        in_specs=[SMEM] + [VMEM] * 4,
        out_specs=(VMEM, VMEM),
        compiler_params=pltpu.CompilerParams(vmem_limit_bytes=4 * MIB),
        cost_estimate=cost(0, 2 * MIB),
        name="choose",
    )(owners, *arrived)


def merge_kernel(owners, own, got, after, out):
    row, side = lax.axis_index("row"), lax.axis_index("col") >> 2
    for tick in range(TICKS):
        part = slice(tick * PROWS, (tick + 1) * PROWS)

        @pl.when(owners[tick, row] >> 2 != side)
        def _():
            out[part, :] = got[part, :]

        @pl.when(owners[tick, row] >> 2 == side)
        def _():
            out[part, :] = own[part, :]


def merge(owners, own, got, after):
    return pl.pallas_call(
        merge_kernel,
        out_shape=jax.ShapeDtypeStruct(own.shape, F32),
        in_specs=[SMEM, VMEM, VMEM, ANY],
        out_specs=VMEM,
        compiler_params=pltpu.CompilerParams(vmem_limit_bytes=4 * MIB),
        cost_estimate=cost(0, MIB),
        name="merge",
    )(owners, own, got, after)


def place(ref, tick, va, tp, base, shift, k):
    at = tick * PROWS
    tiles = pltpu.roll(ref[at : at + VROWS, :].reshape(VROWS // 8, 8, BLOCK), shift, 1)
    same = lax.broadcasted_iota(jnp.int32, (VROWS // 8 - 1, 8, BLOCK), 1) >= shift
    spot = base + k * VROWS
    inner = jnp.where(same, tiles[1:], tiles[:-1]).reshape(VROWS - 8, BLOCK)
    va[tick, pl.ds(pl.multiple_of(spot + 8, 8), VROWS - 8), :] = inner
    zero = jnp.zeros((8, BLOCK), F32)
    first = pl.ds(pl.multiple_of(spot, 8), 8)
    va[tick, first, :] = va[tick, first, :] + jnp.where(same[0], tiles[0], zero)
    last = pl.ds(pl.multiple_of(spot + VROWS, 8), 8)
    va[tick, last, :] = va[tick, last, :] + jnp.where(same[0], zero, tiles[-1])
    tp[tick, pl.ds(pl.multiple_of(k * TROWS, 8), TROWS), :] = ref[at + VROWS : at + PROWS, :]


def spots(col):
    x, here = col & 3, col >> 2
    columns = [2 * ((x + d) & 3) for d in (0, 1, 3, 2)]
    return [c + here for c in columns] + [c + 1 - here for c in columns]


def starts(offsets, row, tick):
    begin = offsets[tick, row] - WIN
    return begin >> 3 << 3, begin & 7


def prepare_kernel(offsets, p, r, l, s, q, va, tp):
    row, col = lax.axis_index("row"), lax.axis_index("col")
    va[...] = jnp.zeros(va.shape, F32)
    for tick in range(TICKS):
        base, shift = starts(offsets, row, tick)
        for ref, k in zip((p, r, l, s, q), spots(col)):
            place(ref, tick, va, tp, base, shift, k)


def prepare(offsets, pieces):
    return pl.pallas_call(
        prepare_kernel,
        out_shape=(
            jax.ShapeDtypeStruct((TICKS, REACH + 16, BLOCK), F32),
            jax.ShapeDtypeStruct((TICKS, PIECES * TROWS, BLOCK), F32),
        ),
        in_specs=[SMEM] + [VMEM] * 5,
        out_specs=(VMEM, VMEM),
        compiler_params=pltpu.CompilerParams(vmem_limit_bytes=8 * MIB),
        cost_estimate=cost(0, 6 * MIB),
        name="prepare",
    )(offsets, *pieces)


def mix(th, tl, coef):
    return mm3(th, tl, *split(coef), NN)


def update_kernel(offsets, wh, wl, low, u, v, z, old, part, bottom, vh, vl, sh, sl, va, tp):
    row, col = lax.axis_index("row"), lax.axis_index("col")
    factors = []
    for tick in range(TICKS):
        base, shift = starts(offsets, row, tick)
        for ref, k in zip((u, v, z), spots(col)[5:]):
            place(ref, tick, va, tp, base, shift, k)
        lanes = slice(tick * BLOCK, (tick + 1) * BLOCK)
        vh[:, lanes], vl[:, lanes] = split(va[tick, :REACH, :])
        packed = tp[tick].reshape(PIECES, TROWS, BLOCK)
        corner = jnp.concatenate([packed[:, 16:, :128].reshape(64, 128), packed[:, 16:, 128:].reshape(64, 128)], 0)
        lower = jnp.concatenate([jnp.zeros((128, 128), F32), corner], 1)
        factors.append(split(jnp.concatenate([packed[:, :16, :].reshape(128, BLOCK), lower], 0)))
    (fh, fl), (gh, gl) = factors
    cross = mm3(vh[:, BLOCK:], vl[:, BLOCK:], vh[:, :BLOCK], vl[:, :BLOCK], TN)
    cross = split(mm3(*split(mix(gh, gl, cross)), fh, fl, NN))
    coef = mm3(vh[...], vl[...], wh[...], wl[...], TN)
    ch, cl = split(coef)
    sh[:BLOCK, :], sl[:BLOCK, :] = split(mm3(fh, fl, ch[:BLOCK], cl[:BLOCK], NN))
    second = mm3(gh, gl, ch[BLOCK:], cl[BLOCK:], NN) - mm3(*cross, ch[:BLOCK], cl[:BLOCK], NN)
    sh[BLOCK:, :], sl[BLOCK:, :] = split(second)
    bottom[...] = low[...] - mm3(vh[WIN:, :], vl[WIN:, :], sh[...], sl[...], NN)


def update(offsets, wh, wl, halo, pieces, va, tp):
    columns = halo.shape[1]
    both = TICKS * BLOCK
    return pl.pallas_call(
        update_kernel,
        out_shape=(
            jax.ShapeDtypeStruct((HALF, columns), F32),
            jax.ShapeDtypeStruct((REACH, both), BF16),
            jax.ShapeDtypeStruct((REACH, both), BF16),
            jax.ShapeDtypeStruct((both, columns), BF16),
            jax.ShapeDtypeStruct((both, columns), BF16),
            jax.ShapeDtypeStruct(va.shape, F32),
            jax.ShapeDtypeStruct(tp.shape, F32),
        ),
        in_specs=[SMEM] + [VMEM] * 8,
        out_specs=(VMEM,) * 7,
        input_output_aliases={7: 5, 8: 6},
        compiler_params=pltpu.CompilerParams(vmem_limit_bytes=24 * MIB),
        cost_estimate=cost(5_000_000_000, 8 * MIB),
        name="update",
    )(offsets, wh, wl, halo, *pieces, va, tp)[:5]


def store_kernel(eig, vh, vl, sh, sl, out, rows, middle, sems):
    count = eig.shape[0]
    spot = pl.ds(HALF, count - WIN - HALF)
    load = pltpu.make_async_copy(eig.at[pl.ds(count - WIN, WIN)], rows, sems.at[0])
    fetch = pltpu.make_async_copy(eig.at[spot], middle, sems.at[1])
    load.start()
    fetch.start()
    fetch.wait()
    keep = pltpu.make_async_copy(middle, out.at[spot], sems.at[2])
    keep.start()
    load.wait()
    for k in range(4):
        part = slice(k * 256, (k + 1) * 256)
        rows[part, :] = rows[part, :] - mm3(vh[part, :], vl[part, :], sh[...], sl[...], NN)
    store = pltpu.make_async_copy(rows, out.at[pl.ds(count - WIN, WIN)], sems.at[3])
    store.start()
    keep.wait()
    store.wait()


def store(eig, vh, vl, sh, sl):
    columns = eig.shape[1]
    return pl.pallas_call(
        store_kernel,
        out_shape=jax.ShapeDtypeStruct(eig.shape, F32),
        in_specs=[HBM] + [VMEM] * 4,
        out_specs=HBM,
        scratch_shapes=[
            pltpu.VMEM((WIN, columns), F32),
            pltpu.VMEM((eig.shape[0] - WIN - HALF, columns), F32),
            pltpu.SemaphoreType.DMA((4,)),
        ],
        compiler_params=pltpu.CompilerParams(vmem_limit_bytes=16 * MIB),
        cost_estimate=cost(1_600_000_000, 8 * MIB),
        name="store",
    )(*hbm(eig), vh, vl, sh, sl)


def finish_kernel(eig, upper, old, out, rows, sems):
    head = out.at[pl.ds(0, HALF)]

    @pl.when(lax.axis_index("row") > 0)
    def _():
        copy = pltpu.make_async_copy(upper, head, sems.at[0])
        copy.start()
        copy.wait()

    @pl.when(lax.axis_index("row") == 0)
    def _():
        fetch = pltpu.make_async_copy(eig.at[pl.ds(0, HALF)], rows, sems.at[1])
        fetch.start()
        fetch.wait()
        copy = pltpu.make_async_copy(rows, head, sems.at[2])
        copy.start()
        copy.wait()


def finish(eig, upper, out):
    return pl.pallas_call(
        finish_kernel,
        out_shape=pltpu.HBM(eig.shape, F32),
        in_specs=[HBM, VMEM, HBM],
        out_specs=HBM,
        input_output_aliases={2: 0},
        scratch_shapes=[pltpu.VMEM((HALF, eig.shape[1]), F32), pltpu.SemaphoreType.DMA((3,))],
        compiler_params=pltpu.CompilerParams(vmem_limit_bytes=4 * MIB),
        cost_estimate=cost(0, 2 * MIB),
        name="finish",
    )(*hbm(eig), *vmem(upper), *hbm(out))


def per_device(eigvec, reflectors, tfactors, offsets, owners):
    count = lax.axis_size("row")

    def from_x(value, d):
        return lax.ppermute(value, "col", [((i // 4) * 4 + (i % 4 + d) % 4, i) for i in range(8)])

    def from_y(value):
        return lax.ppermute(value, "col", [(i, i ^ 4) for i in range(8)])

    stay, right, across, left, top = pack(reflectors, tfactors, eigvec)
    halo = lax.ppermute(top, "row", [(i + 1, i) for i in range(count - 1)])
    far, near, back = from_x(across, 2), from_x(left, 1), from_x(right, -1)
    own, send = choose(owners, (stay, near, far, back))
    got = from_y(send)
    wh, wl = stage(eigvec, halo)
    p = merge(owners, own, got, wh)
    q, s, r, l = from_y(p), from_x(p, 2), from_x(p, 1), from_x(p, -1)
    u, v, z = from_x(q, 1), from_x(q, -1), from_y(s)

    bottom, *rest = update(offsets, wh, wl, halo, (u, v, z), *prepare(offsets, (p, r, l, s, q)))
    upper = lax.ppermute(bottom, "row", [(i, i + 1) for i in range(count - 1)])
    return finish(eigvec, upper, store(eigvec, *rest))


def solution(mesh):
    return jax.shard_map(
        per_device,
        mesh=mesh,
        in_specs=(
            P("row", "col"),
            P("row", "col", None, None),
            P("row", "col", None, None),
            P(),
            P(),
        ),
        out_specs=P("row", "col"),
        check_vma=False,
    )
```

```python
import jax
import jax.numpy as jnp
from jax import lax
from jax.experimental import pallas as pl
from jax.experimental.pallas import tpu as pltpu
from jax.sharding import PartitionSpec as P

WIN = 1024
HALF = 512
BLOCK = 256
TICKS = 2
PIECES = 8
VROWS = WIN // PIECES
TROWS = 24
PROWS = VROWS + TROWS
SPAN = WIN + 16
REACH = WIN + HALF
MIB = 1024 * 1024
F32 = jnp.float32
BF16 = jnp.bfloat16
NN = ((1,), (0,))
TN = ((0,), (0,))

SMEM = pl.BlockSpec(memory_space=pltpu.SMEM)
VMEM = pl.BlockSpec(memory_space=pltpu.VMEM)
ANY = pl.BlockSpec(memory_space=pl.ANY)
HBM = pl.BlockSpec(memory_space=pltpu.HBM)


def split(x):
    hi = x.astype(BF16)
    return hi, (x - hi.astype(F32)).astype(BF16)


def mm(a, b, dims):
    return lax.dot_general(a, b, (dims, ((), ())), preferred_element_type=F32)


def mm3(ah, al, bh, bl, dims):
    return mm(ah, bh, dims) + mm(ah, bl, dims) + mm(al, bh, dims)


def hbm(*arrays):
    return [pltpu.with_memory_space_constraint(a, pltpu.HBM) for a in arrays]


def vmem(*arrays):
    return [pltpu.with_memory_space_constraint(a, pltpu.VMEM) for a in arrays]


def cost(flops, moved):
    return pl.CostEstimate(flops=flops, bytes_accessed=moved, transcendentals=0)


def pack_kernel(vectors, factor, eig, *refs):
    outs, (top, sems, first) = refs[:8], refs[8:]
    col = lax.axis_index("col")
    x, side = col & 3, col >> 2
    copies = []
    for half in range(2):
        for n in range(4):
            k = 2 * ((x + n) & 3) + (1 - side if half == 0 else side)
            out = outs[4 * half + n]
            pairs = (
                (vectors.at[0, 0, pl.ds(pl.multiple_of(k * VROWS, 8), VROWS)], out.at[pl.ds(0, VROWS)]),
                (factor.at[0, 0, pl.ds(pl.multiple_of(k * 16, 8), 16)], out.at[pl.ds(VROWS, 16)]),
                (
                    factor.at[0, 0, pl.ds(pl.multiple_of(128 + k * 8, 8), 8), pl.ds(128, 128)],
                    out.at[pl.ds(VROWS + 16, 8), pl.ds(0, 128)],
                ),
                (
                    factor.at[0, 0, pl.ds(pl.multiple_of(192 + k * 8, 8), 8), pl.ds(128, 128)],
                    out.at[pl.ds(VROWS + 16, 8), pl.ds(128, 128)],
                ),
            )
            for i, (src, dst) in enumerate(pairs):
                copies.append(pltpu.make_async_copy(src, dst, sems.at[n, half, i]))
    for copy in copies:
        copy.start()
    lead = pltpu.make_async_copy(eig.at[pl.ds(0, HALF)], top, first)
    lead.start()
    for copy in copies:
        copy.wait()
    lead.wait()


def pack(reflectors, tfactors, eig):
    piece = jax.ShapeDtypeStruct((PROWS, BLOCK), F32)
    return pl.pallas_call(
        pack_kernel,
        out_shape=(piece,) * 8 + (jax.ShapeDtypeStruct((HALF, eig.shape[1]), F32),),
        in_specs=[HBM, HBM, HBM],
        out_specs=(VMEM,) * 9,
        scratch_shapes=[pltpu.SemaphoreType.DMA((4, 2, 4)), pltpu.SemaphoreType.DMA],
        compiler_params=pltpu.CompilerParams(vmem_limit_bytes=6 * MIB),
        cost_estimate=cost(0, 5 * MIB),
        name="pack",
    )(*hbm(reflectors, tfactors, eig))


def stage_kernel(eig, halo, wh, wl, rows, sems):
    upper = pltpu.make_async_copy(eig.at[pl.ds(eig.shape[0] - WIN, WIN)], rows.at[pl.ds(0, WIN)], sems.at[0])
    lower = pltpu.make_async_copy(halo, rows.at[pl.ds(WIN, HALF)], sems.at[1])
    upper.start()
    lower.start()
    upper.wait()
    lower.wait()
    wh[...], wl[...] = split(rows[...])


def stage(eig, halo):
    columns = eig.shape[1]
    return pl.pallas_call(
        stage_kernel,
        out_shape=(jax.ShapeDtypeStruct((REACH, columns), BF16), jax.ShapeDtypeStruct((REACH, columns), BF16)),
        in_specs=[HBM, ANY],
        out_specs=(VMEM, VMEM),
        scratch_shapes=[pltpu.VMEM((REACH, columns), F32), pltpu.SemaphoreType.DMA((2,))],
        compiler_params=pltpu.CompilerParams(vmem_limit_bytes=10 * MIB),
        cost_estimate=cost(0, MIB // 4),
        name="stage",
    )(*hbm(eig), halo)


def choose_kernel(owners, stay, near, far, back, send):
    row, col = lax.axis_index("row"), lax.axis_index("col")
    for tick in range(TICKS):
        step = (owners[tick, row] - col) & 3
        part = slice(tick * PROWS, (tick + 1) * PROWS)
        for n, ref in enumerate((stay, near, far, back)):

            @pl.when(step == n)
            def _():
                send[part, :] = ref[...]


def choose(owners, arrived):
    return pl.pallas_call(
        choose_kernel,
        out_shape=jax.ShapeDtypeStruct((TICKS * PROWS, BLOCK), F32),
        in_specs=[SMEM] + [VMEM] * 4,
        out_specs=VMEM,
        compiler_params=pltpu.CompilerParams(vmem_limit_bytes=4 * MIB),
        cost_estimate=cost(0, MIB),
        name="choose",
    )(owners, *arrived)


def merge_kernel(owners, stay, near, far, back, got, after, out):
    row, col = lax.axis_index("row"), lax.axis_index("col")
    for tick in range(TICKS):
        owner = owners[tick, row]
        step, same = (owner - col) & 3, owner >> 2 == col >> 2
        part = slice(tick * PROWS, (tick + 1) * PROWS)

        @pl.when(jnp.logical_not(same))
        def _():
            out[part, :] = got[part, :]

        for n, ref in enumerate((stay, near, far, back)):

            @pl.when(jnp.logical_and(same, step == n))
            def _():
                out[part, :] = ref[...]


def merge(owners, arrived, got, after):
    return pl.pallas_call(
        merge_kernel,
        out_shape=jax.ShapeDtypeStruct(got.shape, F32),
        in_specs=[SMEM] + [VMEM] * 5 + [ANY],
        out_specs=VMEM,
        compiler_params=pltpu.CompilerParams(vmem_limit_bytes=4 * MIB),
        cost_estimate=cost(0, MIB),
        name="merge",
    )(owners, *arrived, got, after)


def place(ref, tick, va, tp, base, shift, k):
    at = tick * PROWS
    tiles = pltpu.roll(ref[at : at + VROWS, :].reshape(VROWS // 8, 8, BLOCK), shift, 1)
    same = lax.broadcasted_iota(jnp.int32, (VROWS // 8 - 1, 8, BLOCK), 1) >= shift
    spot = base + k * VROWS
    inner = jnp.where(same, tiles[1:], tiles[:-1]).reshape(VROWS - 8, BLOCK)
    va[tick, pl.ds(pl.multiple_of(spot + 8, 8), VROWS - 8), :] = inner
    zero = jnp.zeros((8, BLOCK), F32)
    first = pl.ds(pl.multiple_of(spot, 8), 8)
    va[tick, first, :] = va[tick, first, :] + jnp.where(same[0], tiles[0], zero)
    last = pl.ds(pl.multiple_of(spot + VROWS, 8), 8)
    va[tick, last, :] = va[tick, last, :] + jnp.where(same[0], zero, tiles[-1])
    tp[tick, pl.ds(pl.multiple_of(k * TROWS, 8), TROWS), :] = ref[at + VROWS : at + PROWS, :]


def spots(col):
    x, here = col & 3, col >> 2
    columns = [2 * ((x + d) & 3) for d in (0, 1, 3, 2)]
    return [c + here for c in columns] + [c + 1 - here for c in columns]


def starts(offsets, row, tick):
    begin = offsets[tick, row] - WIN
    return begin >> 3 << 3, begin & 7


def prepare_kernel(offsets, p, r, l, s, q, va, tp):
    row, col = lax.axis_index("row"), lax.axis_index("col")
    va[...] = jnp.zeros(va.shape, F32)
    for tick in range(TICKS):
        base, shift = starts(offsets, row, tick)
        for ref, k in zip((p, r, l, s, q), spots(col)):
            place(ref, tick, va, tp, base, shift, k)


def prepare(offsets, pieces):
    return pl.pallas_call(
        prepare_kernel,
        out_shape=(
            jax.ShapeDtypeStruct((TICKS, REACH + 16, BLOCK), F32),
            jax.ShapeDtypeStruct((TICKS, PIECES * TROWS, BLOCK), F32),
        ),
        in_specs=[SMEM] + [VMEM] * 5,
        out_specs=(VMEM, VMEM),
        compiler_params=pltpu.CompilerParams(vmem_limit_bytes=8 * MIB),
        cost_estimate=cost(0, 6 * MIB),
        name="prepare",
    )(offsets, *pieces)


def mix(th, tl, coef):
    return mm3(th, tl, *split(coef), NN)


def update_kernel(offsets, wh, wl, low, u, v, z, old, part, bottom, vh, vl, sh, sl, va, tp):
    row, col = lax.axis_index("row"), lax.axis_index("col")
    factors = []
    for tick in range(TICKS):
        base, shift = starts(offsets, row, tick)
        for ref, k in zip((u, v, z), spots(col)[5:]):
            place(ref, tick, va, tp, base, shift, k)
        lanes = slice(tick * BLOCK, (tick + 1) * BLOCK)
        vh[:, lanes], vl[:, lanes] = split(va[tick, :REACH, :])
        packed = tp[tick].reshape(PIECES, TROWS, BLOCK)
        corner = jnp.concatenate([packed[:, 16:, :128].reshape(64, 128), packed[:, 16:, 128:].reshape(64, 128)], 0)
        lower = jnp.concatenate([jnp.zeros((128, 128), F32), corner], 1)
        factors.append(split(jnp.concatenate([packed[:, :16, :].reshape(128, BLOCK), lower], 0)))
    (fh, fl), (gh, gl) = factors
    cross = mm3(vh[:, BLOCK:], vl[:, BLOCK:], vh[:, :BLOCK], vl[:, :BLOCK], TN)
    cross = split(mm3(*split(mix(gh, gl, cross)), fh, fl, NN))
    coef = mm3(vh[...], vl[...], wh[...], wl[...], TN)
    ch, cl = split(coef)
    sh[:BLOCK, :], sl[:BLOCK, :] = split(mm3(fh, fl, ch[:BLOCK], cl[:BLOCK], NN))
    second = mm3(gh, gl, ch[BLOCK:], cl[BLOCK:], NN) - mm3(*cross, ch[:BLOCK], cl[:BLOCK], NN)
    sh[BLOCK:, :], sl[BLOCK:, :] = split(second)
    bottom[...] = low[...] - mm3(vh[WIN:, :], vl[WIN:, :], sh[...], sl[...], NN)


def update(offsets, wh, wl, halo, pieces, va, tp):
    columns = halo.shape[1]
    both = TICKS * BLOCK
    return pl.pallas_call(
        update_kernel,
        out_shape=(
            jax.ShapeDtypeStruct((HALF, columns), F32),
            jax.ShapeDtypeStruct((REACH, both), BF16),
            jax.ShapeDtypeStruct((REACH, both), BF16),
            jax.ShapeDtypeStruct((both, columns), BF16),
            jax.ShapeDtypeStruct((both, columns), BF16),
            jax.ShapeDtypeStruct(va.shape, F32),
            jax.ShapeDtypeStruct(tp.shape, F32),
        ),
        in_specs=[SMEM] + [VMEM] * 8,
        out_specs=(VMEM,) * 7,
        input_output_aliases={7: 5, 8: 6},
        compiler_params=pltpu.CompilerParams(vmem_limit_bytes=24 * MIB),
        cost_estimate=cost(5_000_000_000, 8 * MIB),
        name="update",
    )(offsets, wh, wl, halo, *pieces, va, tp)[:5]


def store_kernel(eig, vh, vl, sh, sl, out, rows, middle, sems):
    count = eig.shape[0]
    spot = pl.ds(HALF, count - WIN - HALF)
    load = pltpu.make_async_copy(eig.at[pl.ds(count - WIN, WIN)], rows, sems.at[0])
    fetch = pltpu.make_async_copy(eig.at[spot], middle, sems.at[1])
    load.start()
    fetch.start()
    fetch.wait()
    keep = pltpu.make_async_copy(middle, out.at[spot], sems.at[2])
    keep.start()
    load.wait()
    for k in range(4):
        part = slice(k * 256, (k + 1) * 256)
        rows[part, :] = rows[part, :] - mm3(vh[part, :], vl[part, :], sh[...], sl[...], NN)
    store = pltpu.make_async_copy(rows, out.at[pl.ds(count - WIN, WIN)], sems.at[3])
    store.start()
    keep.wait()
    store.wait()


def store(eig, vh, vl, sh, sl):
    columns = eig.shape[1]
    return pl.pallas_call(
        store_kernel,
        out_shape=jax.ShapeDtypeStruct(eig.shape, F32),
        in_specs=[HBM] + [VMEM] * 4,
        out_specs=HBM,
        scratch_shapes=[
            pltpu.VMEM((WIN, columns), F32),
            pltpu.VMEM((eig.shape[0] - WIN - HALF, columns), F32),
            pltpu.SemaphoreType.DMA((4,)),
        ],
        compiler_params=pltpu.CompilerParams(vmem_limit_bytes=16 * MIB),
        cost_estimate=cost(1_600_000_000, 8 * MIB),
        name="store",
    )(*hbm(eig), vh, vl, sh, sl)


def finish_kernel(eig, upper, old, out, rows, sems):
    head = out.at[pl.ds(0, HALF)]

    @pl.when(lax.axis_index("row") > 0)
    def _():
        copy = pltpu.make_async_copy(upper, head, sems.at[0])
        copy.start()
        copy.wait()

    @pl.when(lax.axis_index("row") == 0)
    def _():
        fetch = pltpu.make_async_copy(eig.at[pl.ds(0, HALF)], rows, sems.at[1])
        fetch.start()
        fetch.wait()
        copy = pltpu.make_async_copy(rows, head, sems.at[2])
        copy.start()
        copy.wait()


def finish(eig, upper, out):
    return pl.pallas_call(
        finish_kernel,
        out_shape=pltpu.HBM(eig.shape, F32),
        in_specs=[HBM, VMEM, HBM],
        out_specs=HBM,
        input_output_aliases={2: 0},
        scratch_shapes=[pltpu.VMEM((HALF, eig.shape[1]), F32), pltpu.SemaphoreType.DMA((3,))],
        compiler_params=pltpu.CompilerParams(vmem_limit_bytes=4 * MIB),
        cost_estimate=cost(0, 2 * MIB),
        name="finish",
    )(*hbm(eig), *vmem(upper), *hbm(out))


def per_device(eigvec, reflectors, tfactors, offsets, owners):
    count = lax.axis_size("row")

    def from_x(value, d):
        return lax.ppermute(value, "col", [((i // 4) * 4 + (i % 4 + d) % 4, i) for i in range(8)])

    def from_y(value):
        return lax.ppermute(value, "col", [(i, i ^ 4) for i in range(8)])

    *blocks, top = pack(reflectors, tfactors, eigvec)

    def ring(stay, right, across, left):
        return stay, from_x(left, 1), from_x(across, 2), from_x(right, -1)

    got = from_y(choose(owners, ring(*blocks[:4])))
    halo = lax.ppermute(top, "row", [(i + 1, i) for i in range(count - 1)])
    wh, wl = stage(eigvec, halo)
    p = merge(owners, ring(*blocks[4:]), got, wh)
    q, s, r, l = from_y(p), from_x(p, 2), from_x(p, 1), from_x(p, -1)
    u, v, z = from_x(q, 1), from_x(q, -1), from_y(s)

    bottom, *rest = update(offsets, wh, wl, halo, (u, v, z), *prepare(offsets, (p, r, l, s, q)))
    upper = lax.ppermute(bottom, "row", [(i, i + 1) for i in range(count - 1)])
    return finish(eigvec, upper, store(eigvec, *rest))


def solution(mesh):
    return jax.shard_map(
        per_device,
        mesh=mesh,
        in_specs=(
            P("row", "col"),
            P("row", "col", None, None),
            P("row", "col", None, None),
            P(),
            P(),
        ),
        out_specs=P("row", "col"),
        check_vma=False,
    )
```

```python
import functools

import jax
import jax.numpy as jnp
from jax import lax
from jax.experimental import pallas as pl
from jax.experimental.pallas import tpu as pltpu
from jax.sharding import PartitionSpec as P

WIN = 1024
HALF = 512
BLOCK = 256
TICKS = 2
PIECES = 8
VROWS = WIN // PIECES
TROWS = 24
PROWS = VROWS + TROWS
SPAN = WIN + 16
REACH = WIN + HALF
COLS = 256
MIB = 1024 * 1024
F32 = jnp.float32
BF16 = jnp.bfloat16
NN = ((1,), (0,))
TN = ((0,), (0,))

SMEM = pl.BlockSpec(memory_space=pltpu.SMEM)
VMEM = pl.BlockSpec(memory_space=pltpu.VMEM)
ANY = pl.BlockSpec(memory_space=pl.ANY)
HBM = pl.BlockSpec(memory_space=pltpu.HBM)


def split(x):
    hi = x.astype(BF16)
    return hi, (x - hi.astype(F32)).astype(BF16)


def mm(a, b, dims):
    return lax.dot_general(a, b, (dims, ((), ())), preferred_element_type=F32)


def mm3(ah, al, bh, bl, dims):
    return mm(ah, bh, dims) + mm(ah, bl, dims) + mm(al, bh, dims)


def hbm(*arrays):
    return [pltpu.with_memory_space_constraint(a, pltpu.HBM) for a in arrays]


def vmem(*arrays):
    return [pltpu.with_memory_space_constraint(a, pltpu.VMEM) for a in arrays]


def cost(flops, moved):
    return pl.CostEstimate(flops=flops, bytes_accessed=moved, transcendentals=0)


def pack_kernel(vectors, factor, eig, *refs):
    outs, (top, sems, first) = refs[:8], refs[8:]
    col = lax.axis_index("col")
    x, side = col & 3, col >> 2
    copies = []
    for half in range(2):
        for n in range(4):
            k = 2 * ((x + n) & 3) + (1 - side if half == 0 else side)
            out = outs[4 * half + n]
            pairs = (
                (vectors.at[0, 0, pl.ds(pl.multiple_of(k * VROWS, 8), VROWS)], out.at[pl.ds(0, VROWS)]),
                (factor.at[0, 0, pl.ds(pl.multiple_of(k * 16, 8), 16)], out.at[pl.ds(VROWS, 16)]),
                (
                    factor.at[0, 0, pl.ds(pl.multiple_of(128 + k * 8, 8), 8), pl.ds(128, 128)],
                    out.at[pl.ds(VROWS + 16, 8), pl.ds(0, 128)],
                ),
                (
                    factor.at[0, 0, pl.ds(pl.multiple_of(192 + k * 8, 8), 8), pl.ds(128, 128)],
                    out.at[pl.ds(VROWS + 16, 8), pl.ds(128, 128)],
                ),
            )
            for i, (src, dst) in enumerate(pairs):
                copies.append(pltpu.make_async_copy(src, dst, sems.at[n, half, i]))
    for copy in copies:
        copy.start()
    lead = pltpu.make_async_copy(eig.at[pl.ds(0, HALF)], top, first)
    lead.start()
    for copy in copies:
        copy.wait()
    lead.wait()


def pack(reflectors, tfactors, eig):
    piece = jax.ShapeDtypeStruct((PROWS, BLOCK), F32)
    return pl.pallas_call(
        pack_kernel,
        out_shape=(piece,) * 8 + (jax.ShapeDtypeStruct((HALF, eig.shape[1]), F32),),
        in_specs=[HBM, HBM, HBM],
        out_specs=(VMEM,) * 9,
        scratch_shapes=[pltpu.SemaphoreType.DMA((4, 2, 4)), pltpu.SemaphoreType.DMA],
        compiler_params=pltpu.CompilerParams(vmem_limit_bytes=6 * MIB),
        cost_estimate=cost(0, 5 * MIB),
        name="pack",
    )(*hbm(reflectors, tfactors, eig))


def stage_kernel(eig, halo, wh, wl, rh, rl, low, lower, rows, sems):
    upper = pltpu.make_async_copy(eig.at[pl.ds(eig.shape[0] - WIN, WIN)], rows.at[pl.ds(0, WIN)], sems.at[0])
    under = pltpu.make_async_copy(halo, rows.at[pl.ds(WIN, HALF)], sems.at[1])
    upper.start()
    under.start()
    upper.wait()
    under.wait()
    wh[...], wl[...] = split(rows[:, :COLS])
    rh[...], rl[...] = split(rows[:, COLS:])
    low[...] = rows[WIN:, :COLS]
    lower[...] = rows[WIN:, COLS:]


def stage(eig, halo):
    split_half = jax.ShapeDtypeStruct((REACH, COLS), BF16)
    low = jax.ShapeDtypeStruct((HALF, COLS), F32)
    wh, wl, rh, rl, *lows = pl.pallas_call(
        stage_kernel,
        out_shape=(split_half,) * 4 + (low,) * 2,
        in_specs=[HBM, ANY],
        out_specs=(VMEM,) * 6,
        scratch_shapes=[pltpu.VMEM((REACH, eig.shape[1]), F32), pltpu.SemaphoreType.DMA((2,))],
        compiler_params=pltpu.CompilerParams(vmem_limit_bytes=12 * MIB),
        cost_estimate=cost(0, MIB // 4),
        name="stage",
    )(*hbm(eig), halo)
    return (wh, rh), (wl, rl), lows


def choose_kernel(owners, stay, near, far, back, send):
    row, col = lax.axis_index("row"), lax.axis_index("col")
    for tick in range(TICKS):
        step = (owners[tick, row] - col) & 3
        part = slice(tick * PROWS, (tick + 1) * PROWS)
        for n, ref in enumerate((stay, near, far, back)):

            @pl.when(step == n)
            def _():
                send[part, :] = ref[...]


def choose(owners, arrived):
    return pl.pallas_call(
        choose_kernel,
        out_shape=jax.ShapeDtypeStruct((TICKS * PROWS, BLOCK), F32),
        in_specs=[SMEM] + [VMEM] * 4,
        out_specs=VMEM,
        compiler_params=pltpu.CompilerParams(vmem_limit_bytes=4 * MIB),
        cost_estimate=cost(0, MIB),
        name="choose",
    )(owners, *arrived)


def merge_kernel(owners, stay, near, far, back, got, after, out):
    row, col = lax.axis_index("row"), lax.axis_index("col")
    for tick in range(TICKS):
        owner = owners[tick, row]
        step, same = (owner - col) & 3, owner >> 2 == col >> 2
        part = slice(tick * PROWS, (tick + 1) * PROWS)

        @pl.when(jnp.logical_not(same))
        def _():
            out[part, :] = got[part, :]

        for n, ref in enumerate((stay, near, far, back)):

            @pl.when(jnp.logical_and(same, step == n))
            def _():
                out[part, :] = ref[...]


def merge(owners, arrived, got, after):
    return pl.pallas_call(
        merge_kernel,
        out_shape=jax.ShapeDtypeStruct(got.shape, F32),
        in_specs=[SMEM] + [VMEM] * 5 + [ANY],
        out_specs=VMEM,
        compiler_params=pltpu.CompilerParams(vmem_limit_bytes=4 * MIB),
        cost_estimate=cost(0, MIB),
        name="merge",
    )(owners, *arrived, got, after)


def place(ref, tick, va, tp, base, shift, k):
    at = tick * PROWS
    tiles = pltpu.roll(ref[at : at + VROWS, :].reshape(VROWS // 8, 8, BLOCK), shift, 1)
    same = lax.broadcasted_iota(jnp.int32, (VROWS // 8 - 1, 8, BLOCK), 1) >= shift
    spot = base + k * VROWS
    inner = jnp.where(same, tiles[1:], tiles[:-1]).reshape(VROWS - 8, BLOCK)
    va[tick, pl.ds(pl.multiple_of(spot + 8, 8), VROWS - 8), :] = inner
    zero = jnp.zeros((8, BLOCK), F32)
    first = pl.ds(pl.multiple_of(spot, 8), 8)
    va[tick, first, :] = va[tick, first, :] + jnp.where(same[0], tiles[0], zero)
    last = pl.ds(pl.multiple_of(spot + VROWS, 8), 8)
    va[tick, last, :] = va[tick, last, :] + jnp.where(same[0], zero, tiles[-1])
    tp[tick, pl.ds(pl.multiple_of(k * TROWS, 8), TROWS), :] = ref[at + VROWS : at + PROWS, :]


def spots(col):
    x, here = col & 3, col >> 2
    columns = [2 * ((x + d) & 3) for d in (0, 1, 3, 2)]
    return [c + here for c in columns] + [c + 1 - here for c in columns]


def starts(offsets, row, tick):
    begin = offsets[tick, row] - WIN
    return begin >> 3 << 3, begin & 7


def prepare_kernel(offsets, p, r, l, s, q, va, tp):
    row, col = lax.axis_index("row"), lax.axis_index("col")
    va[...] = jnp.zeros(va.shape, F32)
    for tick in range(TICKS):
        base, shift = starts(offsets, row, tick)
        for ref, k in zip((p, r, l, s, q), spots(col)):
            place(ref, tick, va, tp, base, shift, k)


def prepare(offsets, pieces):
    return pl.pallas_call(
        prepare_kernel,
        out_shape=(
            jax.ShapeDtypeStruct((TICKS, REACH + 16, BLOCK), F32),
            jax.ShapeDtypeStruct((TICKS, PIECES * TROWS, BLOCK), F32),
        ),
        in_specs=[SMEM] + [VMEM] * 5,
        out_specs=(VMEM, VMEM),
        compiler_params=pltpu.CompilerParams(vmem_limit_bytes=8 * MIB),
        cost_estimate=cost(0, 6 * MIB),
        name="prepare",
    )(offsets, *pieces)


def mix(th, tl, coef):
    return mm3(th, tl, *split(coef), NN)


def window(offsets, row, tick):
    begin = jnp.minimum((offsets[tick, row] - WIN) >> 4 << 4, REACH - SPAN)
    return pl.ds(pl.multiple_of(begin, 16), SPAN)


def solve(windows, vh, vl, wh, wl, low, factors, bottom, sh, sl):
    (fh, fl), (gh, gl), cross = factors
    lanes = (slice(0, BLOCK), slice(BLOCK, 2 * BLOCK))
    coef = [mm3(vh[w, part], vl[w, part], wh[w, :], wl[w, :], TN) for w, part in zip(windows, lanes)]
    (ch, cl), (dh, dl) = split(coef[0]), split(coef[1])
    sh[:BLOCK, :], sl[:BLOCK, :] = split(mm3(fh, fl, ch, cl, NN))
    second = mm3(gh, gl, dh, dl, NN) - mm3(*cross, ch, cl, NN)
    sh[BLOCK:, :], sl[BLOCK:, :] = split(second)
    bottom[...] = low[...] - mm3(vh[WIN:, :], vl[WIN:, :], sh[...], sl[...], NN)


def first_kernel(offsets, wh, wl, low, u, v, z, old, part, bottom, vh, vl, sh, sl, mh, ml, va, tp):
    row, col = lax.axis_index("row"), lax.axis_index("col")
    factors = []
    for tick in range(TICKS):
        base, shift = starts(offsets, row, tick)
        for ref, k in zip((u, v, z), spots(col)[5:]):
            place(ref, tick, va, tp, base, shift, k)
        lanes = slice(tick * BLOCK, (tick + 1) * BLOCK)
        vh[:, lanes], vl[:, lanes] = split(va[tick, :REACH, :])
        packed = tp[tick].reshape(PIECES, TROWS, BLOCK)
        corner = jnp.concatenate([packed[:, 16:, :128].reshape(64, 128), packed[:, 16:, 128:].reshape(64, 128)], 0)
        lower = jnp.concatenate([jnp.zeros((128, 128), F32), corner], 1)
        factors.append(split(jnp.concatenate([packed[:, :16, :].reshape(128, BLOCK), lower], 0)))
    (fh, fl), (gh, gl) = factors
    windows = [window(offsets, row, tick) for tick in range(TICKS)]
    w = windows[0]
    cross = mm3(vh[w, BLOCK:], vl[w, BLOCK:], vh[w, :BLOCK], vl[w, :BLOCK], TN)
    factors.append(split(mm3(*split(mix(gh, gl, cross)), fh, fl, NN)))
    for n, (hi, lo) in enumerate(factors):
        mh[n], ml[n] = hi, lo
    solve(windows, vh, vl, wh, wl, low, factors, bottom, sh, sl)


def second_kernel(offsets, wh, wl, low, vh, vl, mh, ml, bottom, sh, sl):
    windows = [window(offsets, lax.axis_index("row"), tick) for tick in range(TICKS)]
    solve(windows, vh, vl, wh, wl, low, [(mh[n], ml[n]) for n in range(3)], bottom, sh, sl)


def update(offsets, wh, wl, halo, pieces, va, tp):
    both = TICKS * BLOCK
    shape = jax.ShapeDtypeStruct
    solved = (shape((HALF, COLS), F32), shape((both, COLS), BF16), shape((both, COLS), BF16))
    bottom, vh, vl, sh, sl, mh, ml, *unused = pl.pallas_call(
        first_kernel,
        out_shape=(
            solved[0],
            shape((REACH, both), BF16),
            shape((REACH, both), BF16),
            *solved[1:],
            shape((3, BLOCK, BLOCK), BF16),
            shape((3, BLOCK, BLOCK), BF16),
            shape(va.shape, F32),
            shape(tp.shape, F32),
        ),
        in_specs=[SMEM] + [VMEM] * 8,
        out_specs=(VMEM,) * 9,
        input_output_aliases={7: 7, 8: 8},
        compiler_params=pltpu.CompilerParams(vmem_limit_bytes=20 * MIB),
        cost_estimate=cost(3_000_000_000, 8 * MIB),
        name="first",
    )(offsets, wh[0], wl[0], halo[0], *pieces, va, tp)
    second = pl.pallas_call(
        second_kernel,
        out_shape=solved,
        in_specs=[SMEM] + [VMEM] * 7,
        out_specs=(VMEM,) * 3,
        compiler_params=pltpu.CompilerParams(vmem_limit_bytes=16 * MIB),
        cost_estimate=cost(3_000_000_000, 8 * MIB),
        name="second",
    )(offsets, wh[1], wl[1], halo[1], vh, vl, mh, ml)
    return (bottom, second[0]), (vh, vl, sh, sl, *second[1:])


def store_kernel(eig, vh, vl, sh, sl, rh, rl, out, rows, middle, sems, last):
    count = eig.shape[0]
    loads, stores = [], []
    for k in range(4):
        there, here = pl.ds(count - WIN + k * 256, 256), pl.ds(k * 256, 256)
        loads.append(pltpu.make_async_copy(eig.at[there], rows.at[here], sems.at[0, k]))
        stores.append(pltpu.make_async_copy(rows.at[here], out.at[there], sems.at[1, k]))
    spot = pl.ds(HALF, count - WIN - HALF)
    fetch = pltpu.make_async_copy(eig.at[spot], middle, last.at[0])
    keep = pltpu.make_async_copy(middle, out.at[spot], last.at[1])
    for copy in loads:
        copy.start()
    fetch.start()
    for k in range(4):
        part = slice(k * 256, (k + 1) * 256)
        loads[k].wait()
        rows[part, :COLS] = rows[part, :COLS] - mm3(vh[part, :], vl[part, :], sh[...], sl[...], NN)
        rows[part, COLS:] = rows[part, COLS:] - mm3(vh[part, :], vl[part, :], rh[...], rl[...], NN)
        stores[k].start()
        if k == 1:
            fetch.wait()
            keep.start()
    keep.wait()
    for copy in stores:
        copy.wait()


def store(eig, *solved):
    columns = eig.shape[1]
    return pl.pallas_call(
        store_kernel,
        out_shape=jax.ShapeDtypeStruct(eig.shape, F32),
        in_specs=[HBM] + [VMEM] * 6,
        out_specs=HBM,
        scratch_shapes=[
            pltpu.VMEM((WIN, columns), F32),
            pltpu.VMEM((eig.shape[0] - WIN - HALF, columns), F32),
            pltpu.SemaphoreType.DMA((2, 4)),
            pltpu.SemaphoreType.DMA((2,)),
        ],
        compiler_params=pltpu.CompilerParams(vmem_limit_bytes=16 * MIB),
        cost_estimate=cost(1_600_000_000, 8 * MIB),
        name="store",
    )(*hbm(eig), *solved)


def finish_kernel(half, eig, upper, old, out, rows, sems):
    spot = (pl.ds(0, HALF), pl.ds(half * COLS, COLS))

    @pl.when(lax.axis_index("row") > 0)
    def _():
        copy = pltpu.make_async_copy(upper, out.at[spot], sems.at[0])
        copy.start()
        copy.wait()

    @pl.when(lax.axis_index("row") == 0)
    def _():
        fetch = pltpu.make_async_copy(eig.at[spot], rows, sems.at[1])
        fetch.start()
        fetch.wait()
        copy = pltpu.make_async_copy(rows, out.at[spot], sems.at[2])
        copy.start()
        copy.wait()


def finish(half, eig, upper, out):
    return pl.pallas_call(
        functools.partial(finish_kernel, half),
        out_shape=pltpu.HBM(eig.shape, F32),
        in_specs=[HBM, VMEM, HBM],
        out_specs=HBM,
        input_output_aliases={2: 0},
        scratch_shapes=[pltpu.VMEM((HALF, COLS), F32), pltpu.SemaphoreType.DMA((3,))],
        compiler_params=pltpu.CompilerParams(vmem_limit_bytes=4 * MIB),
        cost_estimate=cost(0, MIB),
        name="finish",
    )(*hbm(eig), *vmem(upper), *hbm(out))


def per_device(eigvec, reflectors, tfactors, offsets, owners):
    count = lax.axis_size("row")

    def from_x(value, d):
        return lax.ppermute(value, "col", [((i // 4) * 4 + (i % 4 + d) % 4, i) for i in range(8)])

    def from_y(value):
        return lax.ppermute(value, "col", [(i, i ^ 4) for i in range(8)])

    *blocks, top = pack(reflectors, tfactors, eigvec)

    def ring(stay, right, across, left):
        return stay, from_x(left, 1), from_x(across, 2), from_x(right, -1)

    got = from_y(choose(owners, ring(*blocks[:4])))
    halo = lax.ppermute(top, "row", [(i + 1, i) for i in range(count - 1)])
    wh, wl, lows = stage(eigvec, halo)
    p = merge(owners, ring(*blocks[4:]), got, wh[0])
    q, s, r, l = from_y(p), from_x(p, 2), from_x(p, 1), from_x(p, -1)
    u, v, z = from_x(q, 1), from_x(q, -1), from_y(s)

    bottoms, solved = update(offsets, wh, wl, lows, (u, v, z), *prepare(offsets, (p, r, l, s, q)))
    result = store(eigvec, *solved)
    for half, bottom in enumerate(bottoms):
        upper = lax.ppermute(bottom, "row", [(i, i + 1) for i in range(count - 1)])
        result = finish(half, eigvec, upper, result)
    return result


def solution(mesh):
    return jax.shard_map(
        per_device,
        mesh=mesh,
        in_specs=(
            P("row", "col"),
            P("row", "col", None, None),
            P("row", "col", None, None),
            P(),
            P(),
        ),
        out_specs=P("row", "col"),
        check_vma=False,
    )
```

```python
import functools

import jax
import jax.numpy as jnp
from jax import lax
from jax.experimental import pallas as pl
from jax.experimental.pallas import tpu as pltpu
from jax.sharding import PartitionSpec as P

WIN = 1024
HALF = 512
BLOCK = 256
TICKS = 2
PIECES = 8
VROWS = WIN // PIECES
TROWS = 24
PROWS = VROWS + TROWS
SPAN = WIN + 16
REACH = WIN + HALF
COLS = 256
MIB = 1024 * 1024
F32 = jnp.float32
BF16 = jnp.bfloat16
NN = ((1,), (0,))
TN = ((0,), (0,))

SMEM = pl.BlockSpec(memory_space=pltpu.SMEM)
VMEM = pl.BlockSpec(memory_space=pltpu.VMEM)
ANY = pl.BlockSpec(memory_space=pl.ANY)
HBM = pl.BlockSpec(memory_space=pltpu.HBM)


def split(x):
    hi = x.astype(BF16)
    return hi, (x - hi.astype(F32)).astype(BF16)


def mm(a, b, dims):
    return lax.dot_general(a, b, (dims, ((), ())), preferred_element_type=F32)


def mm3(ah, al, bh, bl, dims):
    return mm(ah, bh, dims) + mm(ah, bl, dims) + mm(al, bh, dims)


def hbm(*arrays):
    return [pltpu.with_memory_space_constraint(a, pltpu.HBM) for a in arrays]


def vmem(*arrays):
    return [pltpu.with_memory_space_constraint(a, pltpu.VMEM) for a in arrays]


def cost(flops, moved):
    return pl.CostEstimate(flops=flops, bytes_accessed=moved, transcendentals=0)


def pack_kernel(vectors, factor, eig, *refs):
    outs, (top, sems, first) = refs[:8], refs[8:]
    col = lax.axis_index("col")
    x, side = col & 3, col >> 2
    copies = []
    for half in range(2):
        for n in range(4):
            k = 2 * ((x + n) & 3) + (1 - side if half == 0 else side)
            out = outs[4 * half + n]
            pairs = (
                (vectors.at[0, 0, pl.ds(pl.multiple_of(k * VROWS, 8), VROWS)], out.at[pl.ds(0, VROWS)]),
                (factor.at[0, 0, pl.ds(pl.multiple_of(k * 16, 8), 16)], out.at[pl.ds(VROWS, 16)]),
                (
                    factor.at[0, 0, pl.ds(pl.multiple_of(128 + k * 8, 8), 8), pl.ds(128, 128)],
                    out.at[pl.ds(VROWS + 16, 8), pl.ds(0, 128)],
                ),
                (
                    factor.at[0, 0, pl.ds(pl.multiple_of(192 + k * 8, 8), 8), pl.ds(128, 128)],
                    out.at[pl.ds(VROWS + 16, 8), pl.ds(128, 128)],
                ),
            )
            for i, (src, dst) in enumerate(pairs):
                copies.append(pltpu.make_async_copy(src, dst, sems.at[n, half, i]))
    for copy in copies:
        copy.start()
    lead = pltpu.make_async_copy(eig.at[pl.ds(0, HALF)], top, first)
    lead.start()
    for copy in copies:
        copy.wait()
    lead.wait()


def pack(reflectors, tfactors, eig):
    piece = jax.ShapeDtypeStruct((PROWS, BLOCK), F32)
    return pl.pallas_call(
        pack_kernel,
        out_shape=(piece,) * 8 + (jax.ShapeDtypeStruct((HALF, eig.shape[1]), F32),),
        in_specs=[HBM, HBM, HBM],
        out_specs=(VMEM,) * 9,
        scratch_shapes=[pltpu.SemaphoreType.DMA((4, 2, 4)), pltpu.SemaphoreType.DMA],
        compiler_params=pltpu.CompilerParams(vmem_limit_bytes=6 * MIB),
        cost_estimate=cost(0, 5 * MIB),
        name="pack",
    )(*hbm(reflectors, tfactors, eig))


def stage_kernel(eig, halo, wh, wl, rh, rl, low, lower, rows, sems):
    upper = pltpu.make_async_copy(eig.at[pl.ds(eig.shape[0] - WIN, WIN)], rows.at[pl.ds(0, WIN)], sems.at[0])
    under = pltpu.make_async_copy(halo, rows.at[pl.ds(WIN, HALF)], sems.at[1])
    upper.start()
    under.start()
    upper.wait()
    under.wait()
    wh[...], wl[...] = split(rows[:, :COLS])
    rh[...], rl[...] = split(rows[:, COLS:])
    low[...] = rows[WIN:, :COLS]
    lower[...] = rows[WIN:, COLS:]


def stage(eig, halo):
    split_half = jax.ShapeDtypeStruct((REACH, COLS), BF16)
    low = jax.ShapeDtypeStruct((HALF, COLS), F32)
    wh, wl, rh, rl, *lows = pl.pallas_call(
        stage_kernel,
        out_shape=(split_half,) * 4 + (low,) * 2,
        in_specs=[HBM, ANY],
        out_specs=(VMEM,) * 6,
        scratch_shapes=[pltpu.VMEM((REACH, eig.shape[1]), F32), pltpu.SemaphoreType.DMA((2,))],
        compiler_params=pltpu.CompilerParams(vmem_limit_bytes=12 * MIB),
        cost_estimate=cost(0, MIB // 4),
        name="stage",
    )(*hbm(eig), halo)
    return (wh, rh), (wl, rl), lows


def choose_kernel(owners, stay, near, far, back, send):
    row, col = lax.axis_index("row"), lax.axis_index("col")
    for tick in range(TICKS):
        step = (owners[tick, row] - col) & 3
        part = slice(tick * PROWS, (tick + 1) * PROWS)
        for n, ref in enumerate((stay, near, far, back)):

            @pl.when(step == n)
            def _():
                send[part, :] = ref[...]


def choose(owners, arrived):
    return pl.pallas_call(
        choose_kernel,
        out_shape=jax.ShapeDtypeStruct((TICKS * PROWS, BLOCK), F32),
        in_specs=[SMEM] + [VMEM] * 4,
        out_specs=VMEM,
        compiler_params=pltpu.CompilerParams(vmem_limit_bytes=4 * MIB),
        cost_estimate=cost(0, MIB),
        name="choose",
    )(owners, *arrived)


def merge_kernel(owners, stay, near, far, back, got, after, out):
    row, col = lax.axis_index("row"), lax.axis_index("col")
    for tick in range(TICKS):
        owner = owners[tick, row]
        step, same = (owner - col) & 3, owner >> 2 == col >> 2
        part = slice(tick * PROWS, (tick + 1) * PROWS)

        @pl.when(jnp.logical_not(same))
        def _():
            out[part, :] = got[part, :]

        for n, ref in enumerate((stay, near, far, back)):

            @pl.when(jnp.logical_and(same, step == n))
            def _():
                out[part, :] = ref[...]


def merge(owners, arrived, got, after):
    return pl.pallas_call(
        merge_kernel,
        out_shape=jax.ShapeDtypeStruct(got.shape, F32),
        in_specs=[SMEM] + [VMEM] * 5 + [ANY],
        out_specs=VMEM,
        compiler_params=pltpu.CompilerParams(vmem_limit_bytes=4 * MIB),
        cost_estimate=cost(0, MIB),
        name="merge",
    )(owners, *arrived, got, after)


def place(ref, tick, va, tp, base, shift, k):
    at = tick * PROWS
    tiles = pltpu.roll(ref[at : at + VROWS, :].reshape(VROWS // 8, 8, BLOCK), shift, 1)
    same = lax.broadcasted_iota(jnp.int32, (VROWS // 8 - 1, 8, BLOCK), 1) >= shift
    spot = base + k * VROWS
    inner = jnp.where(same, tiles[1:], tiles[:-1]).reshape(VROWS - 8, BLOCK)
    va[tick, pl.ds(pl.multiple_of(spot + 8, 8), VROWS - 8), :] = inner
    zero = jnp.zeros((8, BLOCK), F32)
    first = pl.ds(pl.multiple_of(spot, 8), 8)
    va[tick, first, :] = va[tick, first, :] + jnp.where(same[0], tiles[0], zero)
    last = pl.ds(pl.multiple_of(spot + VROWS, 8), 8)
    va[tick, last, :] = va[tick, last, :] + jnp.where(same[0], zero, tiles[-1])
    tp[tick, pl.ds(pl.multiple_of(k * TROWS, 8), TROWS), :] = ref[at + VROWS : at + PROWS, :]


def spots(col):
    x, here = col & 3, col >> 2
    columns = [2 * ((x + d) & 3) for d in (0, 1, 3, 2)]
    return [c + here for c in columns] + [c + 1 - here for c in columns]


def starts(offsets, row, tick):
    begin = offsets[tick, row] - WIN
    return begin >> 3 << 3, begin & 7


def prepare_kernel(offsets, p, r, l, s, q, va, tp):
    row, col = lax.axis_index("row"), lax.axis_index("col")
    va[...] = jnp.zeros(va.shape, F32)
    for tick in range(TICKS):
        base, shift = starts(offsets, row, tick)
        for ref, k in zip((p, r, l, s, q), spots(col)):
            place(ref, tick, va, tp, base, shift, k)


def prepare(offsets, pieces):
    return pl.pallas_call(
        prepare_kernel,
        out_shape=(
            jax.ShapeDtypeStruct((TICKS, REACH + 16, BLOCK), F32),
            jax.ShapeDtypeStruct((TICKS, PIECES * TROWS, BLOCK), F32),
        ),
        in_specs=[SMEM] + [VMEM] * 5,
        out_specs=(VMEM, VMEM),
        compiler_params=pltpu.CompilerParams(vmem_limit_bytes=8 * MIB),
        cost_estimate=cost(0, 6 * MIB),
        name="prepare",
    )(offsets, *pieces)


def mix(th, tl, coef):
    return mm3(th, tl, *split(coef), NN)


def window(offsets, row, tick):
    begin = jnp.minimum((offsets[tick, row] - WIN) >> 4 << 4, REACH - SPAN)
    return pl.ds(pl.multiple_of(begin, 16), SPAN)


def solve(windows, vh, vl, wh, wl, low, factors, bottom, sh, sl):
    (fh, fl), (gh, gl), cross = factors
    lanes = (slice(0, BLOCK), slice(BLOCK, 2 * BLOCK))
    coef = [mm3(vh[w, part], vl[w, part], wh[w, :], wl[w, :], TN) for w, part in zip(windows, lanes)]
    (ch, cl), (dh, dl) = split(coef[0]), split(coef[1])
    sh[:BLOCK, :], sl[:BLOCK, :] = split(mm3(fh, fl, ch, cl, NN))
    second = mm3(gh, gl, dh, dl, NN) - mm3(*cross, ch, cl, NN)
    sh[BLOCK:, :], sl[BLOCK:, :] = split(second)
    bottom[...] = low[...] - mm3(vh[WIN:, :], vl[WIN:, :], sh[...], sl[...], NN)


def first_kernel(offsets, wh, wl, low, u, v, z, old, part, bottom, vh, vl, sh, sl, mh, ml, va, tp):
    row, col = lax.axis_index("row"), lax.axis_index("col")
    factors = []
    for tick in range(TICKS):
        base, shift = starts(offsets, row, tick)
        for ref, k in zip((u, v, z), spots(col)[5:]):
            place(ref, tick, va, tp, base, shift, k)
        lanes = slice(tick * BLOCK, (tick + 1) * BLOCK)
        vh[:, lanes], vl[:, lanes] = split(va[tick, :REACH, :])
        packed = tp[tick].reshape(PIECES, TROWS, BLOCK)
        corner = jnp.concatenate([packed[:, 16:, :128].reshape(64, 128), packed[:, 16:, 128:].reshape(64, 128)], 0)
        lower = jnp.concatenate([jnp.zeros((128, 128), F32), corner], 1)
        factors.append(split(jnp.concatenate([packed[:, :16, :].reshape(128, BLOCK), lower], 0)))
    (fh, fl), (gh, gl) = factors
    windows = [window(offsets, row, tick) for tick in range(TICKS)]
    w = windows[0]
    cross = mm3(vh[w, BLOCK:], vl[w, BLOCK:], vh[w, :BLOCK], vl[w, :BLOCK], TN)
    factors.append(split(mm3(*split(mix(gh, gl, cross)), fh, fl, NN)))
    for n, (hi, lo) in enumerate(factors):
        mh[n], ml[n] = hi, lo
    solve(windows, vh, vl, wh, wl, low, factors, bottom, sh, sl)


def second_kernel(offsets, wh, wl, low, vh, vl, mh, ml, bottom, sh, sl):
    windows = [window(offsets, lax.axis_index("row"), tick) for tick in range(TICKS)]
    solve(windows, vh, vl, wh, wl, low, [(mh[n], ml[n]) for n in range(3)], bottom, sh, sl)


def update(offsets, wh, wl, halo, pieces, va, tp):
    both = TICKS * BLOCK
    shape = jax.ShapeDtypeStruct
    solved = (shape((HALF, COLS), F32), shape((both, COLS), BF16), shape((both, COLS), BF16))
    bottom, vh, vl, sh, sl, mh, ml, *unused = pl.pallas_call(
        first_kernel,
        out_shape=(
            solved[0],
            shape((REACH, both), BF16),
            shape((REACH, both), BF16),
            *solved[1:],
            shape((3, BLOCK, BLOCK), BF16),
            shape((3, BLOCK, BLOCK), BF16),
            shape(va.shape, F32),
            shape(tp.shape, F32),
        ),
        in_specs=[SMEM] + [VMEM] * 8,
        out_specs=(VMEM,) * 9,
        input_output_aliases={7: 7, 8: 8},
        compiler_params=pltpu.CompilerParams(vmem_limit_bytes=20 * MIB),
        cost_estimate=cost(3_000_000_000, 8 * MIB),
        name="first",
    )(offsets, wh[0], wl[0], halo[0], *pieces, va, tp)
    second = pl.pallas_call(
        second_kernel,
        out_shape=solved,
        in_specs=[SMEM] + [VMEM] * 7,
        out_specs=(VMEM,) * 3,
        compiler_params=pltpu.CompilerParams(vmem_limit_bytes=16 * MIB),
        cost_estimate=cost(3_000_000_000, 8 * MIB),
        name="second",
    )(offsets, wh[1], wl[1], halo[1], vh, vl, mh, ml)
    return (bottom, second[0]), (vh, vl, sh, sl, *second[1:])


def store_kernel(eig, vh, vl, sh, sl, rh, rl, out, rows, middle, sems, last):
    count = eig.shape[0]
    loads, stores = [], []
    for k in range(4):
        there, here = pl.ds(count - WIN + k * 256, 256), pl.ds(k * 256, 256)
        loads.append(pltpu.make_async_copy(eig.at[there], rows.at[here], sems.at[0, k]))
        stores.append(pltpu.make_async_copy(rows.at[here], out.at[there], sems.at[1, k]))
    spot = pl.ds(HALF, count - WIN - HALF)
    fetch = pltpu.make_async_copy(eig.at[spot], middle, last.at[0])
    keep = pltpu.make_async_copy(middle, out.at[spot], last.at[1])
    for copy in loads:
        copy.start()
    fetch.start()
    for k in range(4):
        part = slice(k * 256, (k + 1) * 256)
        loads[k].wait()
        rows[part, :COLS] = rows[part, :COLS] - mm3(vh[part, :], vl[part, :], sh[...], sl[...], NN)
        rows[part, COLS:] = rows[part, COLS:] - mm3(vh[part, :], vl[part, :], rh[...], rl[...], NN)
        stores[k].start()
        if k == 1:
            fetch.wait()
            keep.start()
    keep.wait()
    for copy in stores:
        copy.wait()


def store(eig, *solved):
    columns = eig.shape[1]
    return pl.pallas_call(
        store_kernel,
        out_shape=jax.ShapeDtypeStruct(eig.shape, F32),
        in_specs=[HBM] + [VMEM] * 6,
        out_specs=HBM,
        scratch_shapes=[
            pltpu.VMEM((WIN, columns), F32),
            pltpu.VMEM((eig.shape[0] - WIN - HALF, columns), F32),
            pltpu.SemaphoreType.DMA((2, 4)),
            pltpu.SemaphoreType.DMA((2,)),
        ],
        compiler_params=pltpu.CompilerParams(vmem_limit_bytes=16 * MIB),
        cost_estimate=cost(1_600_000_000, 8 * MIB),
        name="store",
    )(*hbm(eig), *solved)


def finish_kernel(half, eig, upper, old, out, rows, sems):
    spot = (pl.ds(0, HALF), pl.ds(half * COLS, COLS))

    @pl.when(lax.axis_index("row") > 0)
    def _():
        copies = []
        for n in range(4):
            part = pl.ds(n * 128, 128)
            copies.append(pltpu.make_async_copy(upper.at[part], out.at[part, pl.ds(half * COLS, COLS)], sems.at[n]))
        for copy in copies:
            copy.start()
        for copy in copies:
            copy.wait()

    @pl.when(lax.axis_index("row") == 0)
    def _():
        fetch = pltpu.make_async_copy(eig.at[spot], rows, sems.at[4])
        fetch.start()
        fetch.wait()
        copy = pltpu.make_async_copy(rows, out.at[spot], sems.at[5])
        copy.start()
        copy.wait()


def finish(half, eig, upper, out):
    return pl.pallas_call(
        functools.partial(finish_kernel, half),
        out_shape=pltpu.HBM(eig.shape, F32),
        in_specs=[HBM, VMEM, HBM],
        out_specs=HBM,
        input_output_aliases={2: 0},
        scratch_shapes=[pltpu.VMEM((HALF, COLS), F32), pltpu.SemaphoreType.DMA((6,))],
        compiler_params=pltpu.CompilerParams(vmem_limit_bytes=4 * MIB),
        cost_estimate=cost(0, MIB),
        name="finish",
    )(*hbm(eig), *vmem(upper), *hbm(out))


def per_device(eigvec, reflectors, tfactors, offsets, owners):
    count = lax.axis_size("row")

    def from_x(value, d):
        return lax.ppermute(value, "col", [((i // 4) * 4 + (i % 4 + d) % 4, i) for i in range(8)])

    def from_y(value):
        return lax.ppermute(value, "col", [(i, i ^ 4) for i in range(8)])

    *blocks, top = pack(reflectors, tfactors, eigvec)

    def ring(stay, right, across, left):
        return stay, from_x(left, 1), from_x(across, 2), from_x(right, -1)

    got = from_y(choose(owners, ring(*blocks[:4])))
    halo = lax.ppermute(top, "row", [(i + 1, i) for i in range(count - 1)])
    wh, wl, lows = stage(eigvec, halo)
    p = merge(owners, ring(*blocks[4:]), got, wh[0])
    q, s, r, l = from_y(p), from_x(p, 2), from_x(p, 1), from_x(p, -1)
    u, v, z = from_x(q, 1), from_x(q, -1), from_y(s)

    bottoms, solved = update(offsets, wh, wl, lows, (u, v, z), *prepare(offsets, (p, r, l, s, q)))
    result = store(eigvec, *solved)
    for half, bottom in enumerate(bottoms):
        upper = lax.ppermute(bottom, "row", [(i, i + 1) for i in range(count - 1)])
        result = finish(half, eigvec, upper, result)
    return result


def solution(mesh):
    return jax.shard_map(
        per_device,
        mesh=mesh,
        in_specs=(
            P("row", "col"),
            P("row", "col", None, None),
            P("row", "col", None, None),
            P(),
            P(),
        ),
        out_specs=P("row", "col"),
        check_vma=False,
    )
```
